32 devices in a mesh: blk: 8 (over z, core), tenant: 4 (over y, x).
Axes of the slice: x: 2, y: 2, z: 4, core: 2. Of those that a mesh axis runs over, the one named last changes fastest.
Arguments:
- history_u: bfloat16 [4, 1024, 4096], P('tenant', 'blk'), may hold values from -6 to 6
- span_gate: bfloat16 [4, 64, 4096], P('tenant', 'blk'), may hold values from -6 to 6
- span_key: bfloat16 [4, 64, 4096], P('tenant', 'blk'), may hold values from -6 to 6
- span_value: bfloat16 [4, 64, 4096], P('tenant', 'blk'), may hold values from -6 to 6
- filter_taps: bfloat16 [1088, 256], P(('blk', 'tenant'))
- skip_bias: bfloat16 [4096], P(('blk', 'tenant')), may hold values from -6 to 6
- lengths: int32 [4], P('tenant'), may hold values from 1 to 1024, as said below
- page_owner: int32 [4, 8, 1], P('tenant'), may hold values from 0 to 7; in each aligned block of 8 rows (0 to 7, 8 to 15, ..., all dimensions but the last counted through in order) at most 2 rows name the same one
Outputs:
- mixed: bfloat16 [4, 64, 4096], P('tenant', 'blk')
- new_pool: bfloat16 [4, 128, 4096], P('tenant', 'blk')
The draws below stay inside these ranges and needn't reach their ends.
Inputs may be any that keep to these rules, and one draw needn't show every extreme that they name: `lengths`: lengths are at least 1, and some tenant uses all 1024 cached positions in every draw. `page_owner`: among the 8 pages of one tenant no device is named more than 2 times, and some device is named exactly 2 times.
All inputs are finite; a program needn't handle non-finite values.
Results may differ from the reference program's by a relative error of at most 0.0044.
Values may be sent and summed in bfloat16 or wider, within the bound.
No kernel may reach another device: no remote copies, remote signals or barrier semaphores. Data moves between devices by JAX's collectives and lax.ppermute only.
A program may use at most 128 MiB of HBM per device.

```python
import math
import jax
import jax.numpy as jnp
import numpy as np
from jax import lax

D = 4096
GROUPS = 256
GSIZE = 16
PAGE = 8
MOST = 2
TENANTS = 4
HIST = 1024
SPAN = 64
FLEN = 1088
NPAGES = 8
POOL = 128
N_BLK = 8


def draw_filter_taps(key, part):
    key_decay, key_values = jax.random.split(jax.random.fold_in(key, 11))
    lag_float = jnp.arange(FLEN, dtype=jnp.float32)[:, None]
    lowest_log = math.log(30.0)
    values = jax.random.normal(key_values, (FLEN, GROUPS), jnp.float32)
    decay_length = jnp.exp(jax.random.uniform(key_decay, (GROUPS,), jnp.float32, lowest_log, math.log(4.0 * FLEN)))
    return (values * jnp.exp(-lag_float / decay_length[None, :]) * jnp.sqrt(2.0 / decay_length[None, :])).astype(jnp.bfloat16)


def draw_lengths(key, part):
    key_values, key_pick = jax.random.split(jax.random.fold_in(key, 23))
    values = jax.random.randint(key_values, (TENANTS,), 1, HIST + 1, dtype=jnp.int32)
    chosen = jax.random.randint(key_pick, (), 0, TENANTS, dtype=jnp.int32)
    return jnp.where(jnp.arange(TENANTS, dtype=jnp.int32) == chosen, jnp.int32(HIST), values)


def steps_of(key, dims, cuts, low, high):
    def one(position, blocks):
        steps = jax.random.uniform(jax.random.fold_in(jax.random.fold_in(key, 6), position), (blocks,), jnp.float32, low / len(cuts), high / len(cuts))
        return jnp.repeat(jnp.exp(steps), dims[position] // blocks).reshape((-1,) + (1,) * (len(dims) - position - 1))

    loudness = one(*cuts[0])
    for cut in cuts[1:]:
        loudness = loudness * one(*cut)
    return loudness


def shared_out(key, own, number, rows, amount, top, limit, skew):
    order = jax.random.permutation(key, amount)
    packed, common = portions_of(amount, rows * top, limit, skew, True), portions_of(amount, rows * top, limit, skew, False)
    places = jnp.arange(amount)

    def named(sizes, offset_by):
        used = int((sizes > 0).sum())
        fixed = max(1, used // 4)
        passed = fixed + (places - fixed + offset_by * (used - fixed)) % max(1, amount - fixed)
        return jnp.zeros((amount,), jnp.int32).at[order[jnp.where(places < fixed, places, passed)]].set(jnp.asarray(sizes, jnp.int32))

    sizes = jnp.where(number % 4 == 0, named(packed, number // 4), named(common, number - number // 4 - 1))
    mixed = jax.random.permutation(jax.random.fold_in(own, 3), amount)
    giver, taker = mixed[0:amount // 2 * 2:2], mixed[1:amount // 2 * 2:2]
    margin = jnp.minimum(sizes[giver] - 1, limit - sizes[taker]) // 2
    margin = jnp.where((giver == order[0]) | (taker == order[0]) | (sizes[taker] == 0), 0, jnp.maximum(margin, 0))
    passed = jax.random.randint(jax.random.fold_in(own, 4), (amount // 2,), 0, 1 << 20) % (margin + 1)
    sizes = sizes.at[giver].add(-passed).at[taker].add(passed)
    labels = jnp.searchsorted(jnp.cumsum(sizes), jnp.arange(rows * top), side="right").astype(jnp.int32)
    grid = labels.reshape(top, rows).T
    grid = grid[jax.random.permutation(jax.random.fold_in(own, 1), rows)]
    offset_by = jax.random.randint(jax.random.fold_in(own, 2), (rows, 1), 0, top)
    return jnp.take_along_axis(grid, (jnp.arange(top)[None, :] + offset_by) % top, axis=1)


def portions_of(number_of, total, most, skew, full):
    portions = [(1 << 20) // math.isqrt(grade ** skew) + 1 for grade in range(1, number_of + 1)]
    largest = most if full else min(most, max(-(-total // number_of), total * portions[0] // sum(portions)))
    least = 1 if total - largest >= number_of - 1 else 0
    given, surplus = [largest] + [least] * (number_of - 1), total - largest - least * (number_of - 1)
    while surplus > 0:
        candidates = [i for i in range(1, number_of) if given[i] < largest] or [i for i in range(1, number_of) if given[i] < most]
        pool, budget = sum([portions[i] for i in candidates]), surplus
        for i in candidates:
            addition = min(most - given[i], max(1, budget * portions[i] // pool), surplus)
            given[i] = given[i] + addition
            surplus = surplus - addition
    return np.array(given)


def scatter_about(own_key, shape, spread, most, cuts=(), held_as=jnp.bfloat16):
    drawn = spread * jax.random.normal(own_key, shape, jnp.float32)
    if cuts:
        drawn = drawn * steps_of(own_key, shape, cuts, -0.22, 0.18)
    return jnp.clip(drawn, -most, most).astype(held_as)


def setup_inputs(seed: int = 0) -> dict:
    streams_of = jax.random.split(jax.random.key(seed), 9)
    history_u = scatter_about(streams_of[0], (TENANTS, HIST, D), 1.0, 6.0, ((0, 4), (1, 8)))
    span_gate = scatter_about(streams_of[1], (TENANTS, SPAN, D), 1.0, 6.0, ((0, 4), (1, 8)))
    span_key = scatter_about(streams_of[2], (TENANTS, SPAN, D), 1.0, 6.0, ((0, 4), (1, 8)))
    span_value = scatter_about(streams_of[3], (TENANTS, SPAN, D), 1.0, 6.0, ((0, 4), (1, 8)))
    filter_taps = draw_filter_taps(jax.random.fold_in(streams_of[8], 71), 0)
    skip_bias = scatter_about(streams_of[5], (D,), 1.0, 6.0, ((0, 32),))
    lengths = draw_lengths(jax.random.fold_in(streams_of[8], 71), 0)
    page_owner_keys = jax.random.split(jax.random.fold_in(streams_of[7], 1), TENANTS * NPAGES // NPAGES)
    page_owner_turns = jax.random.permutation(jax.random.fold_in(streams_of[7], 3), TENANTS * NPAGES // NPAGES)
    page_owner = jax.vmap(lambda own, number: shared_out(jax.random.fold_in(streams_of[7], 2), own, number, NPAGES, N_BLK, 1, MOST, 2))(page_owner_keys, page_owner_turns).reshape((TENANTS, NPAGES, 1))
    return dict(history_u=history_u, span_gate=span_gate, span_key=span_key, span_value=span_value, filter_taps=filter_taps, skip_bias=skip_bias, lengths=lengths, page_owner=page_owner)


def one_tenant(inputs):
    history, gate_rows, key_rows, value_rows, length, owners, filter_taps, skip_bias = inputs
    conv_input = (key_rows.astype(jnp.float32) * value_rows.astype(jnp.float32)).astype(jnp.bfloat16)
    positions = jnp.arange(HIST, dtype=jnp.int32)
    masked = jnp.where(positions[:, None] < length, history.astype(jnp.float32), jnp.float32(0.0))
    sequence = jnp.concatenate([masked, jnp.zeros((SPAN, D), jnp.float32)], axis=0)
    sequence = lax.dynamic_update_slice(sequence, conv_input.astype(jnp.float32), (length.astype(jnp.int32), jnp.int32(0)))
    fft_length = 1
    while fft_length < 2 * (HIST + SPAN):
        fft_length = fft_length * 2
    channel_block = min(512, D)
    block_count = D // channel_block
    group_block = channel_block // GSIZE
    taps_float = filter_taps.astype(jnp.float32)

    def one_block(block_index):
        taps = lax.dynamic_slice_in_dim(taps_float, block_index * group_block, group_block, 1)
        taps = jnp.repeat(taps, GSIZE, axis=1)
        signal = lax.dynamic_slice_in_dim(sequence, block_index * channel_block, channel_block, 1)
        filter_freq = jnp.fft.rfft(taps, n=fft_length, axis=0)
        signal_freq = jnp.fft.rfft(signal, n=fft_length, axis=0)
        circular = jnp.fft.irfft(filter_freq * signal_freq, n=fft_length, axis=0)
        return lax.dynamic_slice_in_dim(circular, length.astype(jnp.int32), SPAN, 0).astype(jnp.float32)

    pieces = lax.map(one_block, jnp.arange(block_count, dtype=jnp.int32))
    convolved = jnp.transpose(pieces, (1, 0, 2)).reshape(SPAN, D)
    mixed = (gate_rows.astype(jnp.float32) * (convolved + skip_bias.astype(jnp.float32)[None, :] * conv_input.astype(jnp.float32))).astype(jnp.bfloat16)
    onehot = (owners[:, None] == jnp.arange(N_BLK, dtype=jnp.int32)[None, :]).astype(jnp.int32)
    before = jnp.cumsum(onehot, axis=0) - onehot
    slot_rank = jnp.sum(before * onehot, axis=1)
    targets = owners * MOST + slot_rank
    pages = conv_input.reshape(NPAGES, PAGE * D)
    new_pool = jnp.zeros((N_BLK * MOST, PAGE * D), jnp.bfloat16).at[targets].set(pages)
    return mixed, new_pool.reshape(POOL, D)


def reference(history_u, span_gate, span_key, span_value, filter_taps, skip_bias, lengths, page_owner):
    def step_tenant(index):
        return one_tenant((history_u[index], span_gate[index], span_key[index], span_value[index], lengths[index], page_owner[index, :, 0], filter_taps, skip_bias))

    mixed, new_pool = lax.map(step_tenant, jnp.arange(TENANTS, dtype=jnp.int32))
    return (mixed, new_pool)
```

```python
import functools

import jax
import jax.numpy as jnp
from jax import lax
from jax.experimental import pallas as pl
from jax.experimental.pallas import tpu as pltpu
from jax.sharding import PartitionSpec as P

PAGE = 8
MOST = 2
LANES = 128

bf16 = jnp.bfloat16
f32 = jnp.float32


def round_up(value, step):
    return -(-value // step) * step


def pack_kernel(n_ten, taps_ref, bias_ref, key_ref, value_ref, send_ref, input_ref):
    n_dev, padded, lanes = send_ref.shape
    rows = taps_ref.shape[0]
    bias = bias_ref[...].astype(f32)
    if bias.shape[1] < lanes:
        bias = jnp.concatenate([bias, jnp.zeros((1, lanes - bias.shape[1]), f32)], axis=1)
    blocks = []
    for half in range(2):
        taps = taps_ref[:, half * lanes : (half + 1) * lanes].astype(f32)
        parts = [taps, bias]
        if padded > rows + 1:
            parts.append(jnp.zeros((padded - rows - 1, lanes), f32))
        blocks.append(jnp.concatenate(parts, axis=0).astype(bf16))
    for dest in range(n_dev):
        send_ref[dest] = blocks[(dest // n_ten) % 2]
    input_ref[...] = (key_ref[...].astype(f32) * value_ref[...].astype(f32)).astype(bf16)


def source_kernel(len_ref, own_ref, peer_ref, own_in_ref, peer_in_ref, out_ref):
    blk = lax.axis_index("blk")
    core = lax.rem(blk, 2)
    rows, width = own_ref.shape
    new = own_in_ref.shape[0]
    start = (blk - core) * rows
    length = len_ref[0]

    def masked(value, first):
        index = first + lax.broadcasted_iota(jnp.int32, (rows, width), 0)
        return jnp.where(index < length, value.astype(f32), 0.0).astype(bf16)

    own_at = pl.multiple_of(core * rows, rows)
    peer_at = pl.multiple_of((1 - core) * rows, rows)
    out_ref[pl.ds(own_at, rows), :] = masked(own_ref[...], start + core * rows)
    out_ref[pl.ds(peer_at, rows), :] = masked(peer_ref[...], start + (1 - core) * rows)
    own_new = own_in_ref[...].astype(f32)
    peer_new = peer_in_ref[...].astype(f32)
    first = jnp.where(core == 0, own_new, peer_new)
    second = jnp.where(core == 0, peer_new, own_new)
    rest = jnp.zeros((LANES - 2 * new, width), f32)
    out_ref[2 * rows :, :] = jnp.concatenate([first, second, rest], axis=0).astype(bf16)


def conv_kernel(fr, span, gsize, len_ref, taps_ref, source_ref, out_ref, history_taps, new_taps):
    n_dev, padded, groups = taps_ref.shape
    rows = source_ref.shape[0] - LANES
    new = 2 * PAGE
    chip = lax.div(lax.axis_index("blk"), 2)
    length = len_ref[0]

    def reversed_taps(top_lag, low_lag, blocks, lanes):
        first = jnp.clip(lax.div(jnp.maximum(low_lag, 0), fr), 0, n_dev - blocks)
        window = taps_ref[pl.ds(first, blocks)].reshape(blocks * padded, groups)
        shape = (blocks, padded, lanes)
        block = lax.broadcasted_iota(jnp.int32, shape, 0)
        row = lax.broadcasted_iota(jnp.int32, shape, 1)
        lane = lax.broadcasted_iota(jnp.int32, shape, 2)
        lag = (first + block) * fr + row
        pick = jnp.where((row < fr) & (lag + lane == top_lag), 1.0, 0.0)
        pick = pick.reshape(blocks * padded, lanes).astype(bf16)
        return lax.dot_general(
            window, pick, (((0,), (0,)), ((), ())), preferred_element_type=f32
        )

    lanes = history_taps.shape[1]
    base = length - chip * rows
    blocks = min(n_dev, -(-(fr - 1 + rows + span - 1) // fr))
    history_taps[...] = reversed_taps(base + span - 1, base - rows + 1, blocks, lanes)
    new_lanes = new_taps.shape[1]
    new_blocks = min(n_dev, -(-span // fr))
    new_taps[...] = reversed_taps(span - 1 - chip * new, 0, new_blocks, new_lanes)

    per = LANES // gsize
    lane_group = lax.broadcasted_iota(jnp.int32, (span, LANES), 1) // gsize

    def chunk(index, carry):
        tiles = []
        for g in range(per):
            at = index * per + g
            line = history_taps[pl.ds(at, 1), :]
            line = jnp.broadcast_to(line, (span, lanes))
            line = pltpu.roll(line, lanes - (span - 1), 1, stride=1, stride_axis=0)
            fresh = new_taps[pl.ds(at, 1), :]
            fresh = jnp.broadcast_to(fresh, (span, new_lanes))
            fresh = pltpu.roll(fresh, new_lanes - (span - 1), 1, stride=1, stride_axis=0)
            tiles.append(
                jnp.concatenate([line[:, :rows], fresh[:, :LANES]], axis=1).astype(bf16)
            )
        toeplitz = jnp.concatenate(tiles, axis=0)
        column = pl.multiple_of(index * LANES, LANES)
        product = jnp.dot(
            toeplitz, source_ref[:, pl.ds(column, LANES)], preferred_element_type=f32
        )
        total = product[:span]
        for g in range(1, per):
            total = jnp.where(lane_group == g, product[g * span : (g + 1) * span], total)
        out_ref[:, pl.ds(column, LANES)] = total.astype(bf16)
        return carry

    lax.fori_loop(0, groups // per, chunk, 0)


def select_kernel(owner_ref, *refs):
    pages, (own_ref, peer_ref) = refs[:-2], refs[-2:]
    blk = lax.axis_index("blk")
    core = lax.rem(blk, 2)
    chip = lax.div(blk, 2)
    n_chip = len(pages)
    own_ref[...] = jnp.zeros_like(own_ref)
    peer_ref[...] = jnp.zeros_like(peer_ref)
    for step, page in enumerate(pages):
        number = 2 * lax.rem(chip + n_chip - step, n_chip) + core
        owner = owner_ref[number]
        rank = jnp.int32(0)
        for other in range(2 * n_chip):
            earlier = (owner_ref[other] == owner) & (other < number)
            rank = rank + earlier.astype(jnp.int32)
        for target, device in ((own_ref, blk), (peer_ref, blk + 1 - 2 * core)):

            @pl.when(owner == device)
            def _(target=target, page=page, rank=rank):
                target[rank] = page[...]


def finish_kernel(parts_ref, gate_ref, input_ref, bias_ref, own_ref, peer_ref, mixed_ref, pool_ref):
    n_blk, _, half = parts_ref.shape
    for core in range(2):
        columns = slice(core * half, (core + 1) * half)
        total = parts_ref[core].astype(f32)
        for chip in range(1, n_blk // 2):
            total = total + parts_ref[2 * chip + core].astype(f32)
        skip = bias_ref[:, columns].astype(f32) * input_ref[:, columns].astype(f32)
        gate = gate_ref[:, columns].astype(f32)
        mixed_ref[:, columns] = (gate * (total + skip)).astype(bf16)
    pool_ref[...] = own_ref[...] + peer_ref[...]


def whole(memory=pltpu.VMEM):
    return pl.BlockSpec(memory_space=memory)


def per_device(
    history_u, span_gate, span_key, span_value, filter_taps, skip_bias, lengths, page_owner
):
    n_blk, n_ten = lax.axis_size("blk"), lax.axis_size("tenant")
    n_dev, n_chip = n_blk * n_ten, n_blk // 2
    history = history_u[0]
    rows, width = history.shape
    half = width // 2
    span_rows = span_key.shape[1]
    span = span_rows * n_blk
    fr, groups = filter_taps.shape
    gsize = width // groups
    padded = round_up(fr + 1, 8)
    bias_width = skip_bias.shape[0]
    swap = [(i, i ^ 1) for i in range(n_blk)]

    send, inputs = pl.pallas_call(
        functools.partial(pack_kernel, n_ten),
        out_shape=(
            jax.ShapeDtypeStruct((n_dev, padded, groups // 2), bf16),
            jax.ShapeDtypeStruct((span_rows, width), bf16),
        ),
        in_specs=[whole()] * 4,
        out_specs=(whole(), whole()),
        name="pack",
    )(filter_taps, skip_bias.reshape(1, bias_width), span_key[0], span_value[0])

    taps = lax.all_to_all(send, ("blk", "tenant"), split_axis=0, concat_axis=0, tiled=True)
    peer_history = lax.ppermute(history, "blk", swap)
    peer_inputs = lax.ppermute(inputs, "blk", swap)
    pages = [inputs]
    for step in range(1, n_chip):
        turn = [(i, (i + 2 * step) % n_blk) for i in range(n_blk)]
        pages.append(lax.ppermute(inputs, "blk", turn))

    def half_block(count):
        return pl.BlockSpec((count, half), lambda i, n: (0, lax.rem(lax.axis_index("blk"), 2)))

    source = pl.pallas_call(
        source_kernel,
        grid_spec=pltpu.PrefetchScalarGridSpec(
            num_scalar_prefetch=1,
            grid=(1,),
            in_specs=[
                half_block(rows),
                half_block(rows),
                half_block(span_rows),
                half_block(span_rows),
            ],
            out_specs=pl.BlockSpec((2 * rows + LANES, half), lambda i, n: (0, 0)),
        ),
        out_shape=jax.ShapeDtypeStruct((2 * rows + LANES, half), bf16),
        name="source",
    )(lengths, history, peer_history, inputs, peer_inputs)

    partial = pl.pallas_call(
        functools.partial(conv_kernel, fr, span, gsize),
        out_shape=jax.ShapeDtypeStruct((span, half), bf16),
        in_specs=[whole(pltpu.SMEM), whole(), whole()],
        out_specs=whole(),
        scratch_shapes=[
            pltpu.VMEM((groups // 2, round_up(2 * rows + span - 1, LANES)), f32),
            pltpu.VMEM((groups // 2, round_up(2 * PAGE + span - 1, LANES)), f32),
        ],
        name="conv",
    )(lengths, taps, source)

    parts = lax.all_to_all(
        partial.reshape(n_blk, span_rows, half), "blk", split_axis=0, concat_axis=0, tiled=True
    )

    slots = jax.ShapeDtypeStruct((MOST, PAGE, width), bf16)
    own_slots, peer_slots = pl.pallas_call(
        select_kernel,
        out_shape=(slots, slots),
        in_specs=[whole(pltpu.SMEM)] + [whole()] * n_chip,
        out_specs=(whole(), whole()),
        name="select",
    )(page_owner.reshape(n_blk), *pages)
    peer_slots = lax.ppermute(peer_slots, "blk", swap)
    bias = taps[:, fr, :bias_width].reshape(1, width)

    mixed, pool = pl.pallas_call(
        finish_kernel,
        out_shape=(jax.ShapeDtypeStruct((span_rows, width), bf16), slots),
        in_specs=[whole()] * 6,
        out_specs=(whole(), whole()),
        name="finish",
    )(parts, span_gate[0], inputs, bias, own_slots, peer_slots)
    return mixed[None], pool.reshape(1, MOST * PAGE, width)


def solution(mesh):
    return jax.shard_map(
        per_device,
        mesh=mesh,
        in_specs=(
            P("tenant", "blk", None),
            P("tenant", "blk", None),
            P("tenant", "blk", None),
            P("tenant", "blk", None),
            P(("blk", "tenant"), None),
            P(("blk", "tenant")),
            P("tenant"),
            P("tenant", None, None),
        ),
        out_specs=(P("tenant", "blk", None), P("tenant", "blk", None)),
        check_vma=False,
    )
```

```python
import functools

import jax
import jax.numpy as jnp
from jax import lax
from jax.experimental import pallas as pl
from jax.experimental.pallas import tpu as pltpu
from jax.sharding import PartitionSpec as P

PAGE = 8
MOST = 2
LANES = 128

bf16 = jnp.bfloat16
f32 = jnp.float32


def round_up(value, step):
    return -(-value // step) * step


def pack_kernel(n_ten, taps_ref, bias_ref, key_ref, value_ref, send_ref, input_ref):
    n_dev, padded, lanes = send_ref.shape
    rows = taps_ref.shape[0]
    bias = bias_ref[...].astype(f32)
    if bias.shape[1] < lanes:
        bias = jnp.concatenate([bias, jnp.zeros((1, lanes - bias.shape[1]), f32)], axis=1)
    blocks = []
    for half in range(2):
        taps = taps_ref[:, half * lanes : (half + 1) * lanes].astype(f32)
        parts = [taps, bias]
        if padded > rows + 1:
            parts.append(jnp.zeros((padded - rows - 1, lanes), f32))
        blocks.append(jnp.concatenate(parts, axis=0).astype(bf16))
    for dest in range(n_dev):
        send_ref[dest] = blocks[(dest // n_ten) % 2]
    input_ref[...] = (key_ref[...].astype(f32) * value_ref[...].astype(f32)).astype(bf16)


def source_kernel(len_ref, own_ref, peer_ref, out_ref):
    blk = lax.axis_index("blk")
    core = lax.rem(blk, 2)
    rows, width = own_ref.shape
    start = (blk - core) * rows
    length = len_ref[0]

    def masked(value, first):
        index = first + lax.broadcasted_iota(jnp.int32, (rows, width), 0)
        return jnp.where(index < length, value.astype(f32), 0.0).astype(bf16)

    own_at = pl.multiple_of(core * rows, rows)
    peer_at = pl.multiple_of((1 - core) * rows, rows)
    out_ref[pl.ds(own_at, rows), :] = masked(own_ref[...], start + core * rows)
    out_ref[pl.ds(peer_at, rows), :] = masked(peer_ref[...], start + (1 - core) * rows)


def reversed_taps(window, first, fr, top_lag, lanes):
    blocks, padded, groups = window.shape
    shape = (blocks, padded, lanes)
    block = lax.broadcasted_iota(jnp.int32, shape, 0)
    row = lax.broadcasted_iota(jnp.int32, shape, 1)
    lane = lax.broadcasted_iota(jnp.int32, shape, 2)
    lag = (first + block) * fr + row
    pick = jnp.where((row < fr) & (lag + lane == top_lag), 1.0, 0.0)
    pick = pick.reshape(blocks * padded, lanes).astype(bf16)
    return lax.dot_general(
        window.reshape(blocks * padded, groups),
        pick,
        (((0,), (0,)), ((), ())),
        preferred_element_type=f32,
    )


def toeplitz_product(taps_ref, first_group, gsize, outputs, depth, source):
    per = LANES // gsize
    lanes = taps_ref.shape[1]
    tiles = []
    for g in range(per):
        line = jnp.broadcast_to(taps_ref[pl.ds(first_group + g, 1), :], (outputs, lanes))
        line = pltpu.roll(line, lanes - (outputs - 1), 1, stride=1, stride_axis=0)
        tiles.append(line[:, :depth])
    matrix = jnp.concatenate(tiles, axis=0).astype(bf16)
    product = jnp.dot(matrix, source, preferred_element_type=f32)
    group = lax.broadcasted_iota(jnp.int32, (outputs, LANES), 1) // gsize
    total = product[:outputs]
    for g in range(1, per):
        total = jnp.where(group == g, product[g * outputs : (g + 1) * outputs], total)
    return total


def conv_kernel(fr, span, gsize, len_ref, taps_ref, source_ref, out_ref, line_ref):
    n_dev, _, groups = taps_ref.shape
    rows = source_ref.shape[0]
    base = len_ref[0] - lax.div(lax.axis_index("blk"), 2) * rows
    blocks = min(n_dev, -(-(fr - 1 + rows + span - 1) // fr))
    low = jnp.maximum(base - rows + 1, 0)
    first = jnp.clip(lax.div(low, fr), 0, n_dev - blocks)
    line_ref[...] = reversed_taps(
        taps_ref[pl.ds(first, blocks)], first, fr, base + span - 1, line_ref.shape[1]
    )
    per = LANES // gsize
    for index in range(groups // per):
        columns = slice(index * LANES, (index + 1) * LANES)
        total = toeplitz_product(
            line_ref, index * per, gsize, span, rows, source_ref[:, columns]
        )
        out_ref[:, columns] = total.astype(bf16)


def gather_kernel(fr, bias_width, _, taps_ref, *refs):
    pages, (stack_ref, head_ref, bias_ref) = refs[:-3], refs[-3:]
    chip = lax.div(lax.axis_index("blk"), 2)
    n_chip = len(pages)
    for step, page in enumerate(pages):
        stack_ref[lax.rem(chip + n_chip - step, n_chip)] = page[...]
    head_ref[...] = taps_ref[: head_ref.shape[0]]
    each = LANES // bias_width
    for index in range(taps_ref.shape[0] // each):
        row = [
            taps_ref[index * each + i, fr : fr + 1, :bias_width].astype(f32) for i in range(each)
        ]
        row = row[0] if each == 1 else jnp.concatenate(row, axis=1)
        bias_ref[:, index * LANES : (index + 1) * LANES] = row


def span_kernel(
    fr,
    gsize,
    owner_ref,
    own_stack_ref,
    peer_stack_ref,
    own_head_ref,
    peer_head_ref,
    input_ref,
    bias_ref,
    extra_ref,
    pool_ref,
    line_ref,
    source_ref,
):
    blk = lax.axis_index("blk")
    core = lax.rem(blk, 2)
    n_chip, page, width = own_stack_ref.shape
    n_blk = 2 * n_chip
    pool_ref[...] = jnp.zeros_like(pool_ref)
    for chip in range(n_chip):
        for stack, side in ((own_stack_ref, core), (peer_stack_ref, 1 - core)):
            number = 2 * chip + side
            value = stack[chip]
            source_ref[number] = value
            owner = owner_ref[number]
            rank = jnp.int32(0)
            for other in range(n_blk):
                earlier = (owner_ref[other] == owner) & (other < number)
                rank = rank + earlier.astype(jnp.int32)

            @pl.when(owner == blk)
            def _(value=value, rank=rank):
                pool_ref[rank] = value

    groups = own_head_ref.shape[2]
    lanes = line_ref.shape[1]
    top_lag = blk * page + page - 1
    for head, side in ((own_head_ref, core), (peer_head_ref, 1 - core)):
        at = pl.multiple_of(side * groups, groups)
        line_ref[pl.ds(at, groups), :] = reversed_taps(head[...], 0, fr, top_lag, lanes)
    per = LANES // gsize
    for index in range(width // LANES):
        columns = slice(index * LANES, (index + 1) * LANES)
        source = source_ref[:, :, columns].reshape(n_blk * page, LANES)
        total = toeplitz_product(line_ref, index * per, gsize, page, n_blk * page, source)
        skip = bias_ref[:, columns] * input_ref[:, columns].astype(f32)
        extra_ref[:, columns] = total + skip


def finish_kernel(parts_ref, gate_ref, extra_ref, mixed_ref):
    n_blk, _, half = parts_ref.shape
    for core in range(2):
        columns = slice(core * half, (core + 1) * half)
        total = extra_ref[:, columns]
        for chip in range(n_blk // 2):
            total = total + parts_ref[2 * chip + core].astype(f32)
        gate = gate_ref[:, columns].astype(f32)
        mixed_ref[:, columns] = (gate * total).astype(bf16)


def whole(memory=pltpu.VMEM):
    return pl.BlockSpec(memory_space=memory)


def limit(mebibytes):
    return pltpu.CompilerParams(vmem_limit_bytes=mebibytes << 20)


def per_device(
    history_u, span_gate, span_key, span_value, filter_taps, skip_bias, lengths, page_owner
):
    n_blk, n_ten = lax.axis_size("blk"), lax.axis_size("tenant")
    n_dev, n_chip = n_blk * n_ten, n_blk // 2
    history = history_u[0]
    rows, width = history.shape
    half = width // 2
    span_rows = span_key.shape[1]
    span = span_rows * n_blk
    fr, groups = filter_taps.shape
    gsize = width // groups
    padded = round_up(fr + 1, 8)
    bias_width = skip_bias.shape[0]
    swap = [(i, i ^ 1) for i in range(n_blk)]

    send, inputs = pl.pallas_call(
        functools.partial(pack_kernel, n_ten),
        out_shape=(
            jax.ShapeDtypeStruct((n_dev, padded, groups // 2), bf16),
            jax.ShapeDtypeStruct((span_rows, width), bf16),
        ),
        in_specs=[whole()] * 4,
        out_specs=(whole(), whole()),
        compiler_params=limit(8),
        name="pack",
    )(filter_taps, skip_bias.reshape(1, bias_width), span_key[0], span_value[0])

    taps = lax.all_to_all(send, ("blk", "tenant"), split_axis=0, concat_axis=0, tiled=True)
    history, inputs = lax.optimization_barrier((history, inputs))
    peer_history = lax.ppermute(history, "blk", swap)
    pages = [inputs]
    for step in range(1, n_chip):
        turn = [(i, (i + 2 * step) % n_blk) for i in range(n_blk)]
        pages.append(lax.ppermute(inputs, "blk", turn))

    def half_block(count):
        return pl.BlockSpec((count, half), lambda i, n: (0, lax.rem(lax.axis_index("blk"), 2)))

    source = pl.pallas_call(
        source_kernel,
        grid_spec=pltpu.PrefetchScalarGridSpec(
            num_scalar_prefetch=1,
            grid=(1,),
            in_specs=[half_block(rows), half_block(rows)],
            out_specs=pl.BlockSpec((2 * rows, half), lambda i, n: (0, 0)),
        ),
        out_shape=jax.ShapeDtypeStruct((2 * rows, half), bf16),
        compiler_params=limit(8),
        name="source",
    )(lengths, history, peer_history)

    partial = pl.pallas_call(
        functools.partial(conv_kernel, fr, span, gsize),
        out_shape=jax.ShapeDtypeStruct((span, half), bf16),
        in_specs=[whole(pltpu.SMEM), whole(), whole()],
        out_specs=whole(),
        scratch_shapes=[pltpu.VMEM((groups // 2, round_up(2 * rows + span - 1, LANES)), f32)],
        compiler_params=limit(16),
        name="conv",
    )(lengths, taps, source)

    parts = lax.all_to_all(
        partial.reshape(n_blk, span_rows, half), "blk", split_axis=0, concat_axis=0, tiled=True
    )

    stack = jax.ShapeDtypeStruct((n_chip, span_rows, width), bf16)
    head = jax.ShapeDtypeStruct((min(n_dev, -(-span // fr)), padded, groups // 2), bf16)
    own_stack, own_head, bias = pl.pallas_call(
        functools.partial(gather_kernel, fr, bias_width),
        out_shape=(stack, head, jax.ShapeDtypeStruct((1, width), f32)),
        in_specs=[whole(pl.ANY)] + [whole()] * (1 + n_chip),
        out_specs=(whole(),) * 3,
        compiler_params=limit(8),
        name="gather",
    )(partial, taps, *pages)
    peer_stack = lax.ppermute(own_stack, "blk", swap)
    peer_head = lax.ppermute(own_head, "blk", swap)

    extra, pool = pl.pallas_call(
        functools.partial(span_kernel, fr, gsize),
        out_shape=(
            jax.ShapeDtypeStruct((span_rows, width), f32),
            jax.ShapeDtypeStruct((MOST, PAGE, width), bf16),
        ),
        in_specs=[whole(pltpu.SMEM)] + [whole()] * 6,
        out_specs=(whole(), whole()),
        scratch_shapes=[
            pltpu.VMEM((groups, round_up(span + PAGE - 1, LANES)), f32),
            pltpu.VMEM((n_blk, span_rows, width), bf16),
        ],
        compiler_params=limit(8),
        name="span",
    )(page_owner.reshape(n_blk), own_stack, peer_stack, own_head, peer_head, inputs, bias)

    mixed = pl.pallas_call(
        finish_kernel,
        out_shape=jax.ShapeDtypeStruct((span_rows, width), bf16),
        in_specs=[whole()] * 3,
        out_specs=whole(),
        compiler_params=limit(8),
        name="finish",
    )(parts, span_gate[0], extra)
    return mixed[None], pool.reshape(1, MOST * PAGE, width)


def solution(mesh):
    return jax.shard_map(
        per_device,
        mesh=mesh,
        in_specs=(
            P("tenant", "blk", None),
            P("tenant", "blk", None),
            P("tenant", "blk", None),
            P("tenant", "blk", None),
            P(("blk", "tenant"), None),
            P(("blk", "tenant")),
            P("tenant"),
            P("tenant", None, None),
        ),
        out_specs=(P("tenant", "blk", None), P("tenant", "blk", None)),
        check_vma=False,
    )
```

```python
import functools

import jax
import jax.numpy as jnp
from jax import lax
from jax.experimental import pallas as pl
from jax.experimental.pallas import tpu as pltpu
from jax.sharding import PartitionSpec as P

PAGE = 8
MOST = 2
LANES = 128

bf16 = jnp.bfloat16
f32 = jnp.float32


def round_up(value, step):
    return -(-value // step) * step


def pack_kernel(n_ten, taps_hbm, bias_hbm, key_hbm, value_hbm, send_ref, input_ref, *scratch):
    held, sems = scratch[:-1], scratch[-1]
    copies = [
        pltpu.make_async_copy(source, target, sems.at[i])
        for i, (source, target) in enumerate(
            zip((taps_hbm, bias_hbm, key_hbm, value_hbm), held, strict=True)
        )
    ]
    for copy in copies:
        copy.start()
    for copy in copies:
        copy.wait()
    taps_ref, bias_ref, key_ref, value_ref = held
    n_dev, padded, lanes = send_ref.shape
    rows = taps_ref.shape[0]
    bias = bias_ref[...].astype(f32)
    if bias.shape[1] < lanes:
        bias = jnp.concatenate([bias, jnp.zeros((1, lanes - bias.shape[1]), f32)], axis=1)
    blocks = []
    for half in range(2):
        taps = taps_ref[:, half * lanes : (half + 1) * lanes].astype(f32)
        parts = [taps, bias]
        if padded > rows + 1:
            parts.append(jnp.zeros((padded - rows - 1, lanes), f32))
        blocks.append(jnp.concatenate(parts, axis=0).astype(bf16))
    for dest in range(n_dev):
        send_ref[dest] = blocks[(dest // n_ten) % 2]
    input_ref[...] = (key_ref[...].astype(f32) * value_ref[...].astype(f32)).astype(bf16)


def source_kernel(len_ref, own_ref, peer_ref, out_ref):
    blk = lax.axis_index("blk")
    core = lax.rem(blk, 2)
    rows, width = own_ref.shape
    start = (blk - core) * rows
    length = len_ref[0]

    def masked(value, first):
        index = first + lax.broadcasted_iota(jnp.int32, (rows, width), 0)
        return jnp.where(index < length, value.astype(f32), 0.0).astype(bf16)

    own_at = pl.multiple_of(core * rows, rows)
    peer_at = pl.multiple_of((1 - core) * rows, rows)
    out_ref[pl.ds(own_at, rows), :] = masked(own_ref[...], start + core * rows)
    out_ref[pl.ds(peer_at, rows), :] = masked(peer_ref[...], start + (1 - core) * rows)


def reversed_taps(window, first, fr, top_lag, lanes):
    blocks, padded, groups = window.shape
    shape = (blocks, padded, lanes)
    block = lax.broadcasted_iota(jnp.int32, shape, 0)
    row = lax.broadcasted_iota(jnp.int32, shape, 1)
    lane = lax.broadcasted_iota(jnp.int32, shape, 2)
    lag = (first + block) * fr + row
    pick = jnp.where((row < fr) & (lag + lane == top_lag), 1.0, 0.0)
    pick = pick.reshape(blocks * padded, lanes).astype(bf16)
    return lax.dot_general(
        window.reshape(blocks * padded, groups),
        pick,
        (((0,), (0,)), ((), ())),
        preferred_element_type=f32,
    )


def toeplitz_product(taps_ref, first_group, gsize, outputs, depth, source):
    per = LANES // gsize
    lanes = taps_ref.shape[1]
    tiles = []
    for g in range(per):
        line = jnp.broadcast_to(taps_ref[pl.ds(first_group + g, 1), :], (outputs, lanes))
        line = pltpu.roll(line, lanes - (outputs - 1), 1, stride=1, stride_axis=0)
        tiles.append(line[:, :depth])
    matrix = jnp.concatenate(tiles, axis=0).astype(bf16)
    product = jnp.dot(matrix, source, preferred_element_type=f32)
    group = lax.broadcasted_iota(jnp.int32, (outputs, LANES), 1) // gsize
    total = product[:outputs]
    for g in range(1, per):
        total = jnp.where(group == g, product[g * outputs : (g + 1) * outputs], total)
    return total


def conv_kernel(fr, span, gsize, len_ref, taps_ref, source_ref, out_ref, line_ref):
    n_dev, _, groups = taps_ref.shape
    rows = source_ref.shape[0]
    base = len_ref[0] - lax.div(lax.axis_index("blk"), 2) * rows
    blocks = min(n_dev, -(-(fr - 1 + rows + span - 1) // fr))
    low = jnp.maximum(base - rows + 1, 0)
    first = jnp.clip(lax.div(low, fr), 0, n_dev - blocks)
    line_ref[...] = reversed_taps(
        taps_ref[pl.ds(first, blocks)], first, fr, base + span - 1, line_ref.shape[1]
    )
    per = LANES // gsize
    for index in range(groups // per):
        columns = slice(index * LANES, (index + 1) * LANES)
        total = toeplitz_product(
            line_ref, index * per, gsize, span, rows, source_ref[:, columns]
        )
        out_ref[:, columns] = total.astype(bf16)


def gather_kernel(fr, bias_width, _, taps_ref, *refs):
    pages, (stack_ref, head_ref, bias_ref) = refs[:-3], refs[-3:]
    chip = lax.div(lax.axis_index("blk"), 2)
    n_chip = len(pages)
    for step, page in enumerate(pages):
        stack_ref[lax.rem(chip + n_chip - step, n_chip)] = page[...]
    head_ref[...] = taps_ref[: head_ref.shape[0]]
    each = LANES // bias_width
    for index in range(taps_ref.shape[0] // each):
        row = [
            taps_ref[index * each + i, fr : fr + 1, :bias_width].astype(f32) for i in range(each)
        ]
        row = row[0] if each == 1 else jnp.concatenate(row, axis=1)
        bias_ref[:, index * LANES : (index + 1) * LANES] = row


def span_kernel(
    fr,
    gsize,
    owner_ref,
    own_stack_ref,
    peer_stack_ref,
    own_head_ref,
    peer_head_ref,
    input_ref,
    bias_ref,
    extra_ref,
    pool_ref,
    line_ref,
    source_ref,
):
    blk = lax.axis_index("blk")
    core = lax.rem(blk, 2)
    n_chip, page, width = own_stack_ref.shape
    n_blk = 2 * n_chip
    pool_ref[...] = jnp.zeros_like(pool_ref)
    for chip in range(n_chip):
        for stack, side in ((own_stack_ref, core), (peer_stack_ref, 1 - core)):
            number = 2 * chip + side
            value = stack[chip]
            source_ref[number] = value
            owner = owner_ref[number]
            rank = jnp.int32(0)
            for other in range(n_blk):
                earlier = (owner_ref[other] == owner) & (other < number)
                rank = rank + earlier.astype(jnp.int32)

            @pl.when(owner == blk)
            def _(value=value, rank=rank):
                pool_ref[rank] = value

    groups = own_head_ref.shape[2]
    lanes = line_ref.shape[1]
    top_lag = blk * page + page - 1
    for head, side in ((own_head_ref, core), (peer_head_ref, 1 - core)):
        at = pl.multiple_of(side * groups, groups)
        line_ref[pl.ds(at, groups), :] = reversed_taps(head[...], 0, fr, top_lag, lanes)
    per = LANES // gsize
    for index in range(width // LANES):
        columns = slice(index * LANES, (index + 1) * LANES)
        source = source_ref[:, :, columns].reshape(n_blk * page, LANES)
        total = toeplitz_product(line_ref, index * per, gsize, page, n_blk * page, source)
        skip = bias_ref[:, columns] * input_ref[:, columns].astype(f32)
        extra_ref[:, columns] = total + skip


def finish_kernel(parts_ref, gate_ref, extra_ref, mixed_ref):
    n_blk, _, half = parts_ref.shape
    for core in range(2):
        columns = slice(core * half, (core + 1) * half)
        total = extra_ref[:, columns]
        for chip in range(n_blk // 2):
            total = total + parts_ref[2 * chip + core].astype(f32)
        gate = gate_ref[:, columns].astype(f32)
        mixed_ref[:, columns] = (gate * total).astype(bf16)


def whole(memory=pltpu.VMEM):
    return pl.BlockSpec(memory_space=memory)


def limit(mebibytes):
    return pltpu.CompilerParams(vmem_limit_bytes=mebibytes << 20)


def per_device(
    history_u, span_gate, span_key, span_value, filter_taps, skip_bias, lengths, page_owner
):
    n_blk, n_ten = lax.axis_size("blk"), lax.axis_size("tenant")
    n_dev, n_chip = n_blk * n_ten, n_blk // 2
    history = history_u[0]
    rows, width = history.shape
    half = width // 2
    span_rows = span_key.shape[1]
    span = span_rows * n_blk
    fr, groups = filter_taps.shape
    gsize = width // groups
    padded = round_up(fr + 1, 8)
    bias_width = skip_bias.shape[0]
    swap = [(i, i ^ 1) for i in range(n_blk)]

    send, inputs = pl.pallas_call(
        functools.partial(pack_kernel, n_ten),
        out_shape=(
            jax.ShapeDtypeStruct((n_dev, padded, groups // 2), bf16),
            jax.ShapeDtypeStruct((span_rows, width), bf16),
        ),
        in_specs=[whole(pltpu.HBM)] * 4,
        out_specs=(whole(), whole()),
        scratch_shapes=[
            pltpu.VMEM((fr, groups), bf16),
            pltpu.VMEM((1, bias_width), bf16),
            pltpu.VMEM((span_rows, width), bf16),
            pltpu.VMEM((span_rows, width), bf16),
            pltpu.SemaphoreType.DMA((4,)),
        ],
        compiler_params=limit(58),
        name="pack",
    )(filter_taps, skip_bias.reshape(1, bias_width), span_key[0], span_value[0])

    taps = lax.all_to_all(send, ("blk", "tenant"), split_axis=0, concat_axis=0, tiled=True)
    history, inputs = lax.optimization_barrier((history, inputs))
    peer_history = lax.ppermute(history, "blk", swap)
    pages = [inputs]
    for step in range(1, n_chip):
        turn = [(i, (i + 2 * step) % n_blk) for i in range(n_blk)]
        pages.append(lax.ppermute(inputs, "blk", turn))

    def half_block(count):
        return pl.BlockSpec((count, half), lambda i, n: (0, lax.rem(lax.axis_index("blk"), 2)))

    source = pl.pallas_call(
        source_kernel,
        grid_spec=pltpu.PrefetchScalarGridSpec(
            num_scalar_prefetch=1,
            grid=(1,),
            in_specs=[half_block(rows), half_block(rows)],
            out_specs=pl.BlockSpec((2 * rows, half), lambda i, n: (0, 0)),
        ),
        out_shape=jax.ShapeDtypeStruct((2 * rows, half), bf16),
        compiler_params=limit(8),
        name="source",
    )(lengths, history, peer_history)

    taps, source, *pages = lax.optimization_barrier((taps, source, *pages))
    partial = pl.pallas_call(
        functools.partial(conv_kernel, fr, span, gsize),
        out_shape=jax.ShapeDtypeStruct((span, half), bf16),
        in_specs=[whole(pltpu.SMEM), whole(), whole()],
        out_specs=whole(),
        scratch_shapes=[pltpu.VMEM((groups // 2, round_up(2 * rows + span - 1, LANES)), f32)],
        compiler_params=limit(16),
        name="conv",
    )(lengths, taps, source)

    parts = lax.all_to_all(
        partial.reshape(n_blk, span_rows, half), "blk", split_axis=0, concat_axis=0, tiled=True
    )

    stack = jax.ShapeDtypeStruct((n_chip, span_rows, width), bf16)
    head = jax.ShapeDtypeStruct((min(n_dev, -(-span // fr)), padded, groups // 2), bf16)
    own_stack, own_head, bias = pl.pallas_call(
        functools.partial(gather_kernel, fr, bias_width),
        out_shape=(stack, head, jax.ShapeDtypeStruct((1, width), f32)),
        in_specs=[whole(pl.ANY)] + [whole()] * (1 + n_chip),
        out_specs=(whole(),) * 3,
        compiler_params=limit(8),
        name="gather",
    )(partial, taps, *pages)
    peer_stack = lax.ppermute(own_stack, "blk", swap)
    peer_head = lax.ppermute(own_head, "blk", swap)

    extra, pool = pl.pallas_call(
        functools.partial(span_kernel, fr, gsize),
        out_shape=(
            jax.ShapeDtypeStruct((span_rows, width), f32),
            jax.ShapeDtypeStruct((MOST, PAGE, width), bf16),
        ),
        in_specs=[whole(pltpu.SMEM)] + [whole()] * 6,
        out_specs=(whole(), whole()),
        scratch_shapes=[
            pltpu.VMEM((groups, round_up(span + PAGE - 1, LANES)), f32),
            pltpu.VMEM((n_blk, span_rows, width), bf16),
        ],
        compiler_params=limit(8),
        name="span",
    )(page_owner.reshape(n_blk), own_stack, peer_stack, own_head, peer_head, inputs, bias)

    mixed = pl.pallas_call(
        finish_kernel,
        out_shape=jax.ShapeDtypeStruct((span_rows, width), bf16),
        in_specs=[whole()] * 3,
        out_specs=whole(),
        compiler_params=limit(8),
        name="finish",
    )(parts, span_gate[0], extra)
    return mixed[None], pool.reshape(1, MOST * PAGE, width)


def solution(mesh):
    return jax.shard_map(
        per_device,
        mesh=mesh,
        in_specs=(
            P("tenant", "blk", None),
            P("tenant", "blk", None),
            P("tenant", "blk", None),
            P("tenant", "blk", None),
            P(("blk", "tenant"), None),
            P(("blk", "tenant")),
            P("tenant"),
            P("tenant", None, None),
        ),
        out_specs=(P("tenant", "blk", None), P("tenant", "blk", None)),
        check_vma=False,
    )
```

```python
import functools

import jax
import jax.numpy as jnp
from jax import lax
from jax.experimental import pallas as pl
from jax.experimental.pallas import tpu as pltpu
from jax.sharding import PartitionSpec as P

PAGE = 8
MOST = 2
LANES = 128

bf16 = jnp.bfloat16
f32 = jnp.float32


def round_up(value, step):
    return -(-value // step) * step


def pack_kernel(n_ten, taps_hbm, bias_hbm, key_hbm, value_hbm, send_ref, input_ref, *scratch):
    held, sems = scratch[:-1], scratch[-1]
    copies = [
        pltpu.make_async_copy(source, target, sems.at[i])
        for i, (source, target) in enumerate(
            zip((taps_hbm, bias_hbm, key_hbm, value_hbm), held, strict=True)
        )
    ]
    for copy in copies:
        copy.start()
    for copy in copies:
        copy.wait()
    taps_ref, bias_ref, key_ref, value_ref = held
    n_dev, padded, lanes = send_ref.shape
    rows = taps_ref.shape[0]
    bias = bias_ref[...].astype(f32)
    if bias.shape[1] < lanes:
        bias = jnp.concatenate([bias, jnp.zeros((1, lanes - bias.shape[1]), f32)], axis=1)
    blocks = []
    for half in range(2):
        taps = taps_ref[:, half * lanes : (half + 1) * lanes].astype(f32)
        parts = [taps, bias]
        if padded > rows + 1:
            parts.append(jnp.zeros((padded - rows - 1, lanes), f32))
        blocks.append(jnp.concatenate(parts, axis=0).astype(bf16))
    for dest in range(n_dev):
        send_ref[dest] = blocks[(dest // n_ten) % 2]
    input_ref[...] = (key_ref[...].astype(f32) * value_ref[...].astype(f32)).astype(bf16)


def source_kernel(len_ref, own_ref, peer_ref, out_ref):
    blk = lax.axis_index("blk")
    core = lax.rem(blk, 2)
    rows, width = own_ref.shape
    start = (blk - core) * rows
    length = len_ref[0]

    def masked(value, first):
        index = first + lax.broadcasted_iota(jnp.int32, (rows, width), 0)
        return jnp.where(index < length, value.astype(f32), 0.0).astype(bf16)

    own_at = pl.multiple_of(core * rows, rows)
    peer_at = pl.multiple_of((1 - core) * rows, rows)
    out_ref[pl.ds(own_at, rows), :] = masked(own_ref[...], start + core * rows)
    out_ref[pl.ds(peer_at, rows), :] = masked(peer_ref[...], start + (1 - core) * rows)


def reversed_taps(window, first, fr, top_lag, lanes):
    blocks, padded, groups = window.shape
    shape = (blocks, padded, lanes)
    block = lax.broadcasted_iota(jnp.int32, shape, 0)
    row = lax.broadcasted_iota(jnp.int32, shape, 1)
    lane = lax.broadcasted_iota(jnp.int32, shape, 2)
    lag = (first + block) * fr + row
    pick = jnp.where((row < fr) & (lag + lane == top_lag), 1.0, 0.0)
    pick = pick.reshape(blocks * padded, lanes).astype(bf16)
    return lax.dot_general(
        window.reshape(blocks * padded, groups),
        pick,
        (((0,), (0,)), ((), ())),
        preferred_element_type=f32,
    )


def toeplitz_product(taps_ref, first_group, gsize, outputs, depth, source):
    per = LANES // gsize
    lanes = taps_ref.shape[1]
    tiles = []
    for g in range(per):
        line = jnp.broadcast_to(taps_ref[pl.ds(first_group + g, 1), :], (outputs, lanes))
        line = pltpu.roll(line, lanes - (outputs - 1), 1, stride=1, stride_axis=0)
        tiles.append(line[:, :depth])
    matrix = jnp.concatenate(tiles, axis=0).astype(bf16)
    product = jnp.dot(matrix, source, preferred_element_type=f32)
    group = lax.broadcasted_iota(jnp.int32, (outputs, LANES), 1) // gsize
    total = product[:outputs]
    for g in range(1, per):
        total = jnp.where(group == g, product[g * outputs : (g + 1) * outputs], total)
    return total


def conv_kernel(fr, span, gsize, len_ref, taps_ref, source_ref, out_ref, line_ref):
    n_dev, _, groups = taps_ref.shape
    rows = source_ref.shape[0]
    base = len_ref[0] - lax.div(lax.axis_index("blk"), 2) * rows
    blocks = min(n_dev, -(-(fr - 1 + rows + span - 1) // fr))
    low = jnp.maximum(base - rows + 1, 0)
    first = jnp.clip(lax.div(low, fr), 0, n_dev - blocks)
    line_ref[...] = reversed_taps(
        taps_ref[pl.ds(first, blocks)], first, fr, base + span - 1, line_ref.shape[1]
    )
    per = LANES // gsize
    for index in range(groups // per):
        columns = slice(index * LANES, (index + 1) * LANES)
        total = toeplitz_product(
            line_ref, index * per, gsize, span, rows, source_ref[:, columns]
        )
        out_ref[:, columns] = total.astype(bf16)


def gather_kernel(fr, bias_width, _, taps_ref, *refs):
    pages, (stack_ref, head_ref, bias_ref) = refs[:-3], refs[-3:]
    chip = lax.div(lax.axis_index("blk"), 2)
    n_chip = len(pages)
    for step, page in enumerate(pages):
        stack_ref[lax.rem(chip + n_chip - step, n_chip)] = page[...]
    head_ref[...] = taps_ref[: head_ref.shape[0]]
    each = LANES // bias_width
    for index in range(taps_ref.shape[0] // each):
        row = [
            taps_ref[index * each + i, fr : fr + 1, :bias_width].astype(f32) for i in range(each)
        ]
        row = row[0] if each == 1 else jnp.concatenate(row, axis=1)
        bias_ref[:, index * LANES : (index + 1) * LANES] = row


def span_kernel(
    fr,
    gsize,
    owner_ref,
    own_stack_ref,
    peer_stack_ref,
    own_head_ref,
    peer_head_ref,
    input_ref,
    bias_ref,
    extra_ref,
    pool_ref,
    line_ref,
    source_ref,
):
    blk = lax.axis_index("blk")
    core = lax.rem(blk, 2)
    n_chip, page, width = own_stack_ref.shape
    n_blk = 2 * n_chip
    pool_ref[...] = jnp.zeros_like(pool_ref)
    for chip in range(n_chip):
        for stack, side in ((own_stack_ref, core), (peer_stack_ref, 1 - core)):
            number = 2 * chip + side
            value = stack[chip]
            source_ref[number] = value
            owner = owner_ref[number]
            rank = jnp.int32(0)
            for other in range(n_blk):
                earlier = (owner_ref[other] == owner) & (other < number)
                rank = rank + earlier.astype(jnp.int32)

            @pl.when(owner == blk)
            def _(value=value, rank=rank):
                pool_ref[rank] = value

    groups = own_head_ref.shape[2]
    lanes = line_ref.shape[1]
    top_lag = blk * page + page - 1
    for head, side in ((own_head_ref, core), (peer_head_ref, 1 - core)):
        at = pl.multiple_of(side * groups, groups)
        line_ref[pl.ds(at, groups), :] = reversed_taps(head[...], 0, fr, top_lag, lanes)
    per = LANES // gsize
    for index in range(width // LANES):
        columns = slice(index * LANES, (index + 1) * LANES)
        source = source_ref[:, :, columns].reshape(n_blk * page, LANES)
        total = toeplitz_product(line_ref, index * per, gsize, page, n_blk * page, source)
        skip = bias_ref[:, columns] * input_ref[:, columns].astype(f32)
        extra_ref[:, columns] = total + skip


def finish_kernel(parts_ref, gate_ref, extra_ref, mixed_ref):
    n_blk, _, half = parts_ref.shape
    for core in range(2):
        columns = slice(core * half, (core + 1) * half)
        total = extra_ref[:, columns]
        for chip in range(n_blk // 2):
            total = total + parts_ref[2 * chip + core].astype(f32)
        gate = gate_ref[:, columns].astype(f32)
        mixed_ref[:, columns] = (gate * total).astype(bf16)


def whole(memory=pltpu.VMEM):
    return pl.BlockSpec(memory_space=memory)


def limit(mebibytes):
    return pltpu.CompilerParams(vmem_limit_bytes=mebibytes << 20)


def per_device(
    history_u, span_gate, span_key, span_value, filter_taps, skip_bias, lengths, page_owner
):
    n_blk, n_ten = lax.axis_size("blk"), lax.axis_size("tenant")
    n_dev, n_chip = n_blk * n_ten, n_blk // 2
    history = history_u[0]
    rows, width = history.shape
    half = width // 2
    span_rows = span_key.shape[1]
    span = span_rows * n_blk
    fr, groups = filter_taps.shape
    gsize = width // groups
    padded = round_up(fr + 1, 8)
    bias_width = skip_bias.shape[0]
    swap = [(i, i ^ 1) for i in range(n_blk)]

    send, inputs = pl.pallas_call(
        functools.partial(pack_kernel, n_ten),
        out_shape=(
            jax.ShapeDtypeStruct((n_dev, padded, groups // 2), bf16),
            jax.ShapeDtypeStruct((span_rows, width), bf16),
        ),
        in_specs=[whole(pltpu.HBM)] * 4,
        out_specs=(whole(), whole()),
        scratch_shapes=[
            pltpu.VMEM((fr, groups), bf16),
            pltpu.VMEM((1, bias_width), bf16),
            pltpu.VMEM((span_rows, width), bf16),
            pltpu.VMEM((span_rows, width), bf16),
            pltpu.SemaphoreType.DMA((4,)),
        ],
        compiler_params=limit(58),
        name="pack",
    )(filter_taps, skip_bias.reshape(1, bias_width), span_key[0], span_value[0])

    taps = lax.all_to_all(send, ("blk", "tenant"), split_axis=0, concat_axis=0, tiled=True)
    peer_history = lax.ppermute(history, "blk", swap)

    def half_block(count):
        return pl.BlockSpec((count, half), lambda i, n: (0, lax.rem(lax.axis_index("blk"), 2)))

    source = pl.pallas_call(
        source_kernel,
        grid_spec=pltpu.PrefetchScalarGridSpec(
            num_scalar_prefetch=1,
            grid=(1,),
            in_specs=[half_block(rows), half_block(rows)],
            out_specs=pl.BlockSpec((2 * rows, half), lambda i, n: (0, 0)),
        ),
        out_shape=jax.ShapeDtypeStruct((2 * rows, half), bf16),
        compiler_params=limit(8),
        name="source",
    )(lengths, history, peer_history)

    source, inputs = lax.optimization_barrier((source, inputs))
    pages = [inputs]
    for step in range(1, n_chip):
        turn = [(i, (i + 2 * step) % n_blk) for i in range(n_blk)]
        pages.append(lax.ppermute(inputs, "blk", turn))
    partial = pl.pallas_call(
        functools.partial(conv_kernel, fr, span, gsize),
        out_shape=jax.ShapeDtypeStruct((span, half), bf16),
        in_specs=[whole(pltpu.SMEM), whole(), whole()],
        out_specs=whole(),
        scratch_shapes=[pltpu.VMEM((groups // 2, round_up(2 * rows + span - 1, LANES)), f32)],
        compiler_params=limit(16),
        name="conv",
    )(lengths, taps, source)

    partial, *pages = lax.optimization_barrier((partial, *pages))
    parts = lax.all_to_all(
        partial.reshape(n_blk, span_rows, half), "blk", split_axis=0, concat_axis=0, tiled=True
    )

    stack = jax.ShapeDtypeStruct((n_chip, span_rows, width), bf16)
    head = jax.ShapeDtypeStruct((min(n_dev, -(-span // fr)), padded, groups // 2), bf16)
    own_stack, own_head, bias = pl.pallas_call(
        functools.partial(gather_kernel, fr, bias_width),
        out_shape=(stack, head, jax.ShapeDtypeStruct((1, width), f32)),
        in_specs=[whole(pl.ANY)] + [whole()] * (1 + n_chip),
        out_specs=(whole(),) * 3,
        compiler_params=limit(8),
        name="gather",
    )(partial, taps, *pages)
    peer_stack = lax.ppermute(own_stack, "blk", swap)
    peer_head = lax.ppermute(own_head, "blk", swap)

    extra, pool = pl.pallas_call(
        functools.partial(span_kernel, fr, gsize),
        out_shape=(
            jax.ShapeDtypeStruct((span_rows, width), f32),
            jax.ShapeDtypeStruct((MOST, PAGE, width), bf16),
        ),
        in_specs=[whole(pltpu.SMEM)] + [whole()] * 6,
        out_specs=(whole(), whole()),
        scratch_shapes=[
            pltpu.VMEM((groups, round_up(span + PAGE - 1, LANES)), f32),
            pltpu.VMEM((n_blk, span_rows, width), bf16),
        ],
        compiler_params=limit(8),
        name="span",
    )(page_owner.reshape(n_blk), own_stack, peer_stack, own_head, peer_head, inputs, bias)

    mixed = pl.pallas_call(
        finish_kernel,
        out_shape=jax.ShapeDtypeStruct((span_rows, width), bf16),
        in_specs=[whole()] * 3,
        out_specs=whole(),
        compiler_params=limit(8),
        name="finish",
    )(parts, span_gate[0], extra)
    return mixed[None], pool.reshape(1, MOST * PAGE, width)


def solution(mesh):
    return jax.shard_map(
        per_device,
        mesh=mesh,
        in_specs=(
            P("tenant", "blk", None),
            P("tenant", "blk", None),
            P("tenant", "blk", None),
            P("tenant", "blk", None),
            P(("blk", "tenant"), None),
            P(("blk", "tenant")),
            P("tenant"),
            P("tenant", None, None),
        ),
        out_specs=(P("tenant", "blk", None), P("tenant", "blk", None)),
        check_vma=False,
    )
```

```python
import functools

import jax
import jax.numpy as jnp
from jax import lax
from jax.experimental import pallas as pl
from jax.experimental.pallas import tpu as pltpu
from jax.sharding import PartitionSpec as P

PAGE = 8
MOST = 2
LANES = 128

bf16 = jnp.bfloat16
f32 = jnp.float32


def round_up(value, step):
    return -(-value // step) * step


def pack_kernel(n_ten, taps_hbm, bias_hbm, send_hbm, token_ref, taps_ref, bias_ref, block_ref, sems):
    n_dev, padded, lanes = send_hbm.shape
    rows = taps_ref.shape[0]
    fetch = [
        pltpu.make_async_copy(taps_hbm, taps_ref, sems.at[0]),
        pltpu.make_async_copy(bias_hbm, bias_ref, sems.at[1]),
    ]
    for copy in fetch:
        copy.start()
    for copy in fetch:
        copy.wait()
    bias = bias_ref[...].astype(f32)
    if bias.shape[1] < lanes:
        bias = jnp.concatenate([bias, jnp.zeros((1, lanes - bias.shape[1]), f32)], axis=1)
    for half in range(2):
        taps = taps_ref[:, half * lanes : (half + 1) * lanes].astype(f32)
        parts = [taps, bias]
        if padded > rows + 1:
            parts.append(jnp.zeros((padded - rows - 1, lanes), f32))
        block_ref[half] = jnp.concatenate(parts, axis=0).astype(bf16)
    copies = [
        pltpu.make_async_copy(block_ref.at[(i // n_ten) % 2], send_hbm.at[i], sems.at[2 + i])
        for i in range(n_dev)
    ]
    for copy in copies:
        copy.start()
    token_ref[...] = jnp.zeros_like(token_ref)
    for copy in copies:
        copy.wait()


def input_kernel(_, key_ref, value_ref, input_ref):
    input_ref[...] = (key_ref[...].astype(f32) * value_ref[...].astype(f32)).astype(bf16)


def source_kernel(len_ref, own_ref, peer_ref, out_ref):
    blk = lax.axis_index("blk")
    core = lax.rem(blk, 2)
    rows, width = own_ref.shape
    start = (blk - core) * rows
    length = len_ref[0]

    def masked(value, first):
        index = first + lax.broadcasted_iota(jnp.int32, (rows, width), 0)
        return jnp.where(index < length, value.astype(f32), 0.0).astype(bf16)

    own_at = pl.multiple_of(core * rows, rows)
    peer_at = pl.multiple_of((1 - core) * rows, rows)
    out_ref[pl.ds(own_at, rows), :] = masked(own_ref[...], start + core * rows)
    out_ref[pl.ds(peer_at, rows), :] = masked(peer_ref[...], start + (1 - core) * rows)


def reversed_taps(window, first, fr, top_lag, lanes):
    blocks, padded, groups = window.shape
    shape = (blocks, padded, lanes)
    block = lax.broadcasted_iota(jnp.int32, shape, 0)
    row = lax.broadcasted_iota(jnp.int32, shape, 1)
    lane = lax.broadcasted_iota(jnp.int32, shape, 2)
    lag = (first + block) * fr + row
    pick = jnp.where((row < fr) & (lag + lane == top_lag), 1.0, 0.0)
    pick = pick.reshape(blocks * padded, lanes).astype(bf16)
    return lax.dot_general(
        window.reshape(blocks * padded, groups),
        pick,
        (((0,), (0,)), ((), ())),
        preferred_element_type=f32,
    )


def toeplitz_product(taps_ref, first_group, gsize, outputs, depth, source):
    per = LANES // gsize
    lanes = taps_ref.shape[1]
    tiles = []
    for g in range(per):
        line = jnp.broadcast_to(taps_ref[pl.ds(first_group + g, 1), :], (outputs, lanes))
        line = pltpu.roll(line, lanes - (outputs - 1), 1, stride=1, stride_axis=0)
        tiles.append(line[:, :depth])
    matrix = jnp.concatenate(tiles, axis=0).astype(bf16)
    product = jnp.dot(matrix, source, preferred_element_type=f32)
    group = lax.broadcasted_iota(jnp.int32, (outputs, LANES), 1) // gsize
    total = product[:outputs]
    for g in range(1, per):
        total = jnp.where(group == g, product[g * outputs : (g + 1) * outputs], total)
    return total


def conv_kernel(fr, span, gsize, len_ref, taps_ref, source_ref, out_ref, line_ref):
    n_dev, _, groups = taps_ref.shape
    rows = source_ref.shape[0]
    base = len_ref[0] - lax.div(lax.axis_index("blk"), 2) * rows
    blocks = min(n_dev, -(-(fr - 1 + rows + span - 1) // fr))
    low = jnp.maximum(base - rows + 1, 0)
    first = jnp.clip(lax.div(low, fr), 0, n_dev - blocks)
    line_ref[...] = reversed_taps(
        taps_ref[pl.ds(first, blocks)], first, fr, base + span - 1, line_ref.shape[1]
    )
    per = LANES // gsize
    for index in range(groups // per):
        columns = slice(index * LANES, (index + 1) * LANES)
        total = toeplitz_product(
            line_ref, index * per, gsize, span, rows, source_ref[:, columns]
        )
        out_ref[:, columns] = total.astype(bf16)


def gather_kernel(fr, bias_width, _, taps_ref, *refs):
    pages, (stack_ref, head_ref, bias_ref) = refs[:-3], refs[-3:]
    chip = lax.div(lax.axis_index("blk"), 2)
    for step, page in enumerate(pages):
        stack_ref[lax.bitwise_xor(chip, step)] = page[...]
    head_ref[...] = taps_ref[: head_ref.shape[0]]
    each = LANES // bias_width
    for index in range(taps_ref.shape[0] // each):
        row = [
            taps_ref[index * each + i, fr : fr + 1, :bias_width].astype(f32) for i in range(each)
        ]
        row = row[0] if each == 1 else jnp.concatenate(row, axis=1)
        bias_ref[:, index * LANES : (index + 1) * LANES] = row


def span_kernel(
    fr,
    gsize,
    owner_ref,
    own_stack_ref,
    peer_stack_ref,
    own_head_ref,
    peer_head_ref,
    input_ref,
    bias_ref,
    extra_ref,
    pool_ref,
    line_ref,
    source_ref,
):
    blk = lax.axis_index("blk")
    core = lax.rem(blk, 2)
    n_chip, page, width = own_stack_ref.shape
    n_blk = 2 * n_chip
    pool_ref[...] = jnp.zeros_like(pool_ref)
    for chip in range(n_chip):
        for stack, side in ((own_stack_ref, core), (peer_stack_ref, 1 - core)):
            number = 2 * chip + side
            value = stack[chip]
            source_ref[number] = value
            owner = owner_ref[number]
            rank = jnp.int32(0)
            for other in range(n_blk):
                earlier = (owner_ref[other] == owner) & (other < number)
                rank = rank + earlier.astype(jnp.int32)

            @pl.when(owner == blk)
            def _(value=value, rank=rank):
                pool_ref[rank] = value

    groups = own_head_ref.shape[2]
    lanes = line_ref.shape[1]
    top_lag = blk * page + page - 1
    for head, side in ((own_head_ref, core), (peer_head_ref, 1 - core)):
        at = pl.multiple_of(side * groups, groups)
        line_ref[pl.ds(at, groups), :] = reversed_taps(head[...], 0, fr, top_lag, lanes)
    per = LANES // gsize
    for index in range(width // LANES):
        columns = slice(index * LANES, (index + 1) * LANES)
        source = source_ref[:, :, columns].reshape(n_blk * page, LANES)
        total = toeplitz_product(line_ref, index * per, gsize, page, n_blk * page, source)
        skip = bias_ref[:, columns] * input_ref[:, columns].astype(f32)
        extra_ref[:, columns] = total + skip


def finish_kernel(parts_ref, gate_ref, extra_ref, mixed_ref):
    n_blk, _, half = parts_ref.shape
    for core in range(2):
        columns = slice(core * half, (core + 1) * half)
        total = extra_ref[:, columns]
        for chip in range(n_blk // 2):
            total = total + parts_ref[2 * chip + core].astype(f32)
        gate = gate_ref[:, columns].astype(f32)
        mixed_ref[:, columns] = (gate * total).astype(bf16)


def whole(memory=pltpu.VMEM):
    return pl.BlockSpec(memory_space=memory)


def limit(mebibytes):
    return pltpu.CompilerParams(vmem_limit_bytes=mebibytes << 20)


def per_device(
    history_u, span_gate, span_key, span_value, filter_taps, skip_bias, lengths, page_owner
):
    n_blk, n_ten = lax.axis_size("blk"), lax.axis_size("tenant")
    n_dev, n_chip = n_blk * n_ten, n_blk // 2
    history = history_u[0]
    rows, width = history.shape
    half = width // 2
    span_rows = span_key.shape[1]
    span = span_rows * n_blk
    fr, groups = filter_taps.shape
    gsize = width // groups
    padded = round_up(fr + 1, 8)
    bias_width = skip_bias.shape[0]
    swap = [(i, i ^ 1) for i in range(n_blk)]

    send, token = pl.pallas_call(
        functools.partial(pack_kernel, n_ten),
        out_shape=(
            jax.ShapeDtypeStruct((n_dev, padded, groups // 2), bf16),
            jax.ShapeDtypeStruct((8, LANES), f32),
        ),
        in_specs=[whole(pltpu.HBM)] * 2,
        out_specs=(whole(pltpu.HBM), whole()),
        scratch_shapes=[
            pltpu.VMEM((fr, groups), bf16),
            pltpu.VMEM((1, bias_width), bf16),
            pltpu.VMEM((2, padded, groups // 2), bf16),
            pltpu.SemaphoreType.DMA((2 + n_dev,)),
        ],
        compiler_params=limit(58),
        name="pack",
    )(filter_taps, skip_bias.reshape(1, bias_width))
    taps = lax.all_to_all(send, ("blk", "tenant"), split_axis=0, concat_axis=0, tiled=True)

    inputs = pl.pallas_call(
        input_kernel,
        out_shape=jax.ShapeDtypeStruct((span_rows, width), bf16),
        in_specs=[whole(pl.ANY)] + [whole()] * 2,
        out_specs=whole(),
        compiler_params=limit(8),
        name="inputs",
    )(token, span_key[0], span_value[0])
    peer_history = lax.ppermute(history, "blk", swap)

    def half_block(count):
        return pl.BlockSpec((count, half), lambda i, n: (0, lax.rem(lax.axis_index("blk"), 2)))

    source = pl.pallas_call(
        source_kernel,
        grid_spec=pltpu.PrefetchScalarGridSpec(
            num_scalar_prefetch=1,
            grid=(1,),
            in_specs=[half_block(rows), half_block(rows)],
            out_specs=pl.BlockSpec((2 * rows, half), lambda i, n: (0, 0)),
        ),
        out_shape=jax.ShapeDtypeStruct((2 * rows, half), bf16),
        compiler_params=limit(8),
        name="source",
    )(lengths, history, peer_history)

    source, inputs = lax.optimization_barrier((source, inputs))
    pages = {0: inputs}
    far = n_chip // 2
    while far:
        across = [(i, i ^ (2 * far)) for i in range(n_blk)]
        pages.update({at ^ far: lax.ppermute(page, "blk", across) for at, page in pages.items()})
        far //= 2
    pages = [pages[at] for at in range(n_chip)]

    partial = pl.pallas_call(
        functools.partial(conv_kernel, fr, span, gsize),
        out_shape=jax.ShapeDtypeStruct((span, half), bf16),
        in_specs=[whole(pltpu.SMEM), whole(), whole()],
        out_specs=whole(),
        scratch_shapes=[pltpu.VMEM((groups // 2, round_up(2 * rows + span - 1, LANES)), f32)],
        compiler_params=limit(16),
        name="conv",
    )(lengths, taps, source)

    partial, *pages = lax.optimization_barrier((partial, *pages))
    parts = lax.all_to_all(
        partial.reshape(n_blk, span_rows, half), "blk", split_axis=0, concat_axis=0, tiled=True
    )

    stack = jax.ShapeDtypeStruct((n_chip, span_rows, width), bf16)
    head = jax.ShapeDtypeStruct((min(n_dev, -(-span // fr)), padded, groups // 2), bf16)
    own_stack, own_head, bias = pl.pallas_call(
        functools.partial(gather_kernel, fr, bias_width),
        out_shape=(stack, head, jax.ShapeDtypeStruct((1, width), f32)),
        in_specs=[whole(pl.ANY)] + [whole()] * (1 + n_chip),
        out_specs=(whole(),) * 3,
        compiler_params=limit(8),
        name="gather",
    )(partial, taps, *pages)
    peer_stack = lax.ppermute(own_stack, "blk", swap)
    peer_head = lax.ppermute(own_head, "blk", swap)

    extra, pool = pl.pallas_call(
        functools.partial(span_kernel, fr, gsize),
        out_shape=(
            jax.ShapeDtypeStruct((span_rows, width), f32),
            jax.ShapeDtypeStruct((MOST, PAGE, width), bf16),
        ),
        in_specs=[whole(pltpu.SMEM)] + [whole()] * 6,
        out_specs=(whole(), whole()),
        scratch_shapes=[
            pltpu.VMEM((groups, round_up(span + PAGE - 1, LANES)), f32),
            pltpu.VMEM((n_blk, span_rows, width), bf16),
        ],
        compiler_params=limit(8),
        name="span",
    )(page_owner.reshape(n_blk), own_stack, peer_stack, own_head, peer_head, inputs, bias)

    mixed = pl.pallas_call(
        finish_kernel,
        out_shape=jax.ShapeDtypeStruct((span_rows, width), bf16),
        in_specs=[whole()] * 3,
        out_specs=whole(),
        compiler_params=limit(8),
        name="finish",
    )(parts, span_gate[0], extra)
    return mixed[None], pool.reshape(1, MOST * PAGE, width)


def solution(mesh):
    return jax.shard_map(
        per_device,
        mesh=mesh,
        in_specs=(
            P("tenant", "blk", None),
            P("tenant", "blk", None),
            P("tenant", "blk", None),
            P("tenant", "blk", None),
            P(("blk", "tenant"), None),
            P(("blk", "tenant")),
            P("tenant"),
            P("tenant", None, None),
        ),
        out_specs=(P("tenant", "blk", None), P("tenant", "blk", None)),
        check_vma=False,
    )
```

```python
import functools

import jax
import jax.numpy as jnp
from jax import lax
from jax.experimental import pallas as pl
from jax.experimental.pallas import tpu as pltpu
from jax.sharding import PartitionSpec as P

PAGE = 8
MOST = 2
LANES = 128

bf16 = jnp.bfloat16
f32 = jnp.float32


def round_up(value, step):
    return -(-value // step) * step


def middle_out(count):
    low, high = list(range(count // 2))[::-1], list(range(count // 2, count))
    return [chip for pair in zip(low, high, strict=True) for chip in pair]


def part_order(n_blk):
    return [2 * chip + core for chip in middle_out(n_blk // 2) for core in (1, 0)]


def tap_order(n_blk, n_ten):
    chips = middle_out(n_blk // 2)
    chips = chips[len(chips) // 2 :] + chips[: len(chips) // 2]
    return [
        (2 * chip + core) * n_ten + tenant
        for core in range(2)
        for chip in chips
        for tenant in range(n_ten)
    ]


def tap_place(number, n_blk, n_ten):
    order = tap_order(n_blk, n_ten)
    block, tenant = lax.div(number, n_ten), lax.rem(number, n_ten)
    core, chip = lax.rem(block, 2), lax.div(block, 2)
    place = jnp.int32(0)
    for each in range(n_blk // 2):
        place = jnp.where(chip == each, order.index(2 * each * n_ten), place)
    return place + core * (len(order) // 2) + tenant


def pack_kernel(order, n_ten, taps_hbm, bias_hbm, key_hbm, value_hbm, send_ref, input_ref, *scratch):
    held, sems = scratch[:-1], scratch[-1]
    copies = [
        pltpu.make_async_copy(source, target, sems.at[i])
        for i, (source, target) in enumerate(
            zip((taps_hbm, bias_hbm, key_hbm, value_hbm), held, strict=True)
        )
    ]
    for copy in copies:
        copy.start()
    for copy in copies:
        copy.wait()
    taps_ref, bias_ref, key_ref, value_ref = held
    n_dev, padded, lanes = send_ref.shape
    rows = taps_ref.shape[0]
    bias = bias_ref[...].astype(f32)
    if bias.shape[1] < lanes:
        bias = jnp.concatenate([bias, jnp.zeros((1, lanes - bias.shape[1]), f32)], axis=1)
    blocks = []
    for half in range(2):
        taps = taps_ref[:, half * lanes : (half + 1) * lanes].astype(f32)
        parts = [taps, bias]
        if padded > rows + 1:
            parts.append(jnp.zeros((padded - rows - 1, lanes), f32))
        blocks.append(jnp.concatenate(parts, axis=0).astype(bf16))
    for place in range(n_dev):
        send_ref[place] = blocks[(order[place] // n_ten) % 2]
    input_ref[...] = (key_ref[...].astype(f32) * value_ref[...].astype(f32)).astype(bf16)


def source_kernel(len_ref, own_ref, peer_ref, out_ref):
    blk = lax.axis_index("blk")
    core = lax.rem(blk, 2)
    rows, width = own_ref.shape
    start = (blk - core) * rows
    length = len_ref[0]

    def masked(value, first):
        index = first + lax.broadcasted_iota(jnp.int32, (rows, width), 0)
        return jnp.where(index < length, value.astype(f32), 0.0).astype(bf16)

    own_at = pl.multiple_of(core * rows, rows)
    peer_at = pl.multiple_of((1 - core) * rows, rows)
    out_ref[pl.ds(own_at, rows), :] = masked(own_ref[...], start + core * rows)
    out_ref[pl.ds(peer_at, rows), :] = masked(peer_ref[...], start + (1 - core) * rows)


def reversed_taps(window, first, fr, top_lag, lanes):
    blocks, padded, groups = window.shape
    shape = (blocks, padded, lanes)
    block = lax.broadcasted_iota(jnp.int32, shape, 0)
    row = lax.broadcasted_iota(jnp.int32, shape, 1)
    lane = lax.broadcasted_iota(jnp.int32, shape, 2)
    lag = (first + block) * fr + row
    pick = jnp.where((row < fr) & (lag + lane == top_lag), 1.0, 0.0)
    pick = pick.reshape(blocks * padded, lanes).astype(bf16)
    return lax.dot_general(
        window.reshape(blocks * padded, groups),
        pick,
        (((0,), (0,)), ((), ())),
        preferred_element_type=f32,
    )


def toeplitz_product(taps_ref, first_group, gsize, outputs, depth, source):
    per = LANES // gsize
    lanes = taps_ref.shape[1]
    tiles = []
    for g in range(per):
        line = jnp.broadcast_to(taps_ref[pl.ds(first_group + g, 1), :], (outputs, lanes))
        line = pltpu.roll(line, lanes - (outputs - 1), 1, stride=1, stride_axis=0)
        tiles.append(line[:, :depth])
    matrix = jnp.concatenate(tiles, axis=0).astype(bf16)
    product = jnp.dot(matrix, source, preferred_element_type=f32)
    group = lax.broadcasted_iota(jnp.int32, (outputs, LANES), 1) // gsize
    total = product[:outputs]
    for g in range(1, per):
        total = jnp.where(group == g, product[g * outputs : (g + 1) * outputs], total)
    return total


def conv_kernel(fr, n_ten, gsize, len_ref, taps_ref, source_ref, out_ref, line_ref):
    n_dev, _, groups = taps_ref.shape
    n_blk, page, _ = out_ref.shape
    span = n_blk * page
    rows = source_ref.shape[0]
    base = len_ref[0] - lax.div(lax.axis_index("blk"), 2) * rows
    blocks = min(n_dev, -(-(fr - 1 + rows + span - 1) // fr))
    low = jnp.maximum(base - rows + 1, 0)
    first = jnp.clip(lax.div(low, fr), 0, n_dev - blocks)
    window = [taps_ref[tap_place(first + i, n_blk, n_ten)] for i in range(blocks)]
    line_ref[...] = reversed_taps(
        jnp.stack(window), first, fr, base + span - 1, line_ref.shape[1]
    )
    per = LANES // gsize
    for index in range(groups // per):
        columns = slice(index * LANES, (index + 1) * LANES)
        total = toeplitz_product(
            line_ref, index * per, gsize, span, rows, source_ref[:, columns]
        )
        for place, block in enumerate(part_order(n_blk)):
            out_ref[place, :, columns] = total[block * page : (block + 1) * page].astype(bf16)


def gather_kernel(order, fr, bias_width, _, taps_ref, *refs):
    pages, (stack_ref, head_ref, bias_ref) = refs[:-3], refs[-3:]
    chip = lax.div(lax.axis_index("blk"), 2)
    n_chip = len(pages)
    for step, page in enumerate(pages):
        stack_ref[lax.rem(chip + n_chip - step, n_chip)] = page[...]
    for index in range(head_ref.shape[0]):
        head_ref[index] = taps_ref[order.index(index)]
    each = LANES // bias_width
    for index in range(taps_ref.shape[0] // each):
        row = [
            taps_ref[order.index(index * each + i), fr : fr + 1, :bias_width].astype(f32)
            for i in range(each)
        ]
        row = row[0] if each == 1 else jnp.concatenate(row, axis=1)
        bias_ref[:, index * LANES : (index + 1) * LANES] = row


def span_kernel(
    fr,
    gsize,
    owner_ref,
    own_stack_ref,
    peer_stack_ref,
    own_head_ref,
    peer_head_ref,
    input_ref,
    bias_ref,
    extra_ref,
    pool_ref,
    line_ref,
    source_ref,
):
    blk = lax.axis_index("blk")
    core = lax.rem(blk, 2)
    n_chip, page, width = own_stack_ref.shape
    n_blk = 2 * n_chip
    pool_ref[...] = jnp.zeros_like(pool_ref)
    for chip in range(n_chip):
        for stack, side in ((own_stack_ref, core), (peer_stack_ref, 1 - core)):
            number = 2 * chip + side
            value = stack[chip]
            source_ref[number] = value
            owner = owner_ref[number]
            rank = jnp.int32(0)
            for other in range(n_blk):
                earlier = (owner_ref[other] == owner) & (other < number)
                rank = rank + earlier.astype(jnp.int32)

            @pl.when(owner == blk)
            def _(value=value, rank=rank):
                pool_ref[rank] = value

    groups = own_head_ref.shape[2]
    lanes = line_ref.shape[1]
    top_lag = blk * page + page - 1
    for head, side in ((own_head_ref, core), (peer_head_ref, 1 - core)):
        at = pl.multiple_of(side * groups, groups)
        line_ref[pl.ds(at, groups), :] = reversed_taps(head[...], 0, fr, top_lag, lanes)
    per = LANES // gsize
    for index in range(width // LANES):
        columns = slice(index * LANES, (index + 1) * LANES)
        source = source_ref[:, :, columns].reshape(n_blk * page, LANES)
        total = toeplitz_product(line_ref, index * per, gsize, page, n_blk * page, source)
        skip = bias_ref[:, columns] * input_ref[:, columns].astype(f32)
        extra_ref[:, columns] = total + skip


def finish_kernel(parts_ref, gate_ref, extra_ref, mixed_ref):
    n_blk, _, half = parts_ref.shape
    for core in range(2):
        columns = slice(core * half, (core + 1) * half)
        total = extra_ref[:, columns]
        for place, block in enumerate(part_order(n_blk)):
            if block % 2 == core:
                total = total + parts_ref[place].astype(f32)
        gate = gate_ref[:, columns].astype(f32)
        mixed_ref[:, columns] = (gate * total).astype(bf16)


def whole(memory=pltpu.VMEM):
    return pl.BlockSpec(memory_space=memory)


def limit(mebibytes):
    return pltpu.CompilerParams(vmem_limit_bytes=mebibytes << 20)


def per_device(
    history_u, span_gate, span_key, span_value, filter_taps, skip_bias, lengths, page_owner
):
    n_blk, n_ten = lax.axis_size("blk"), lax.axis_size("tenant")
    n_dev, n_chip = n_blk * n_ten, n_blk // 2
    history = history_u[0]
    rows, width = history.shape
    half = width // 2
    span_rows = span_key.shape[1]
    span = span_rows * n_blk
    fr, groups = filter_taps.shape
    gsize = width // groups
    padded = round_up(fr + 1, 8)
    bias_width = skip_bias.shape[0]
    swap = [(i, i ^ 1) for i in range(n_blk)]

    send, inputs = pl.pallas_call(
        functools.partial(pack_kernel, tap_order(n_blk, n_ten), n_ten),
        out_shape=(
            jax.ShapeDtypeStruct((n_dev, padded, groups // 2), bf16),
            jax.ShapeDtypeStruct((span_rows, width), bf16),
        ),
        in_specs=[whole(pltpu.HBM)] * 4,
        out_specs=(whole(), whole()),
        scratch_shapes=[
            pltpu.VMEM((fr, groups), bf16),
            pltpu.VMEM((1, bias_width), bf16),
            pltpu.VMEM((span_rows, width), bf16),
            pltpu.VMEM((span_rows, width), bf16),
            pltpu.SemaphoreType.DMA((4,)),
        ],
        compiler_params=limit(58),
        name="pack",
    )(filter_taps, skip_bias.reshape(1, bias_width), span_key[0], span_value[0])

    taps = lax.all_to_all(
        send,
        ("blk", "tenant"),
        split_axis=0,
        concat_axis=0,
        axis_index_groups=[tap_order(n_blk, n_ten)],
        tiled=True,
    )
    peer_history = lax.ppermute(history, "blk", swap)

    def half_block(count):
        return pl.BlockSpec((count, half), lambda i, n: (0, lax.rem(lax.axis_index("blk"), 2)))

    source = pl.pallas_call(
        source_kernel,
        grid_spec=pltpu.PrefetchScalarGridSpec(
            num_scalar_prefetch=1,
            grid=(1,),
            in_specs=[half_block(rows), half_block(rows)],
            out_specs=pl.BlockSpec((2 * rows, half), lambda i, n: (0, 0)),
        ),
        out_shape=jax.ShapeDtypeStruct((2 * rows, half), bf16),
        compiler_params=limit(8),
        name="source",
    )(lengths, history, peer_history)

    source, inputs = lax.optimization_barrier((source, inputs))
    pages = [inputs]
    for step in range(1, n_chip):
        turn = [(i, (i + 2 * step) % n_blk) for i in range(n_blk)]
        pages.append(lax.ppermute(inputs, "blk", turn))
    partial = pl.pallas_call(
        functools.partial(conv_kernel, fr, n_ten, gsize),
        out_shape=jax.ShapeDtypeStruct((n_blk, span_rows, half), bf16),
        in_specs=[whole(pltpu.SMEM), whole(), whole()],
        out_specs=whole(),
        scratch_shapes=[pltpu.VMEM((groups // 2, round_up(2 * rows + span - 1, LANES)), f32)],
        compiler_params=limit(16),
        name="conv",
    )(lengths, taps, source)

    partial, *pages = lax.optimization_barrier((partial, *pages))
    parts = lax.all_to_all(
        partial,
        "blk",
        split_axis=0,
        concat_axis=0,
        axis_index_groups=[part_order(n_blk)],
        tiled=True,
    )

    stack = jax.ShapeDtypeStruct((n_chip, span_rows, width), bf16)
    head = jax.ShapeDtypeStruct((min(n_dev, -(-span // fr)), padded, groups // 2), bf16)
    own_stack, own_head, bias = pl.pallas_call(
        functools.partial(gather_kernel, tap_order(n_blk, n_ten), fr, bias_width),
        out_shape=(stack, head, jax.ShapeDtypeStruct((1, width), f32)),
        in_specs=[whole(pl.ANY)] + [whole()] * (1 + n_chip),
        out_specs=(whole(),) * 3,
        compiler_params=limit(8),
        name="gather",
    )(partial, taps, *pages)
    peer_stack = lax.ppermute(own_stack, "blk", swap)
    peer_head = lax.ppermute(own_head, "blk", swap)

    extra, pool = pl.pallas_call(
        functools.partial(span_kernel, fr, gsize),
        out_shape=(
            jax.ShapeDtypeStruct((span_rows, width), f32),
            jax.ShapeDtypeStruct((MOST, PAGE, width), bf16),
        ),
        in_specs=[whole(pltpu.SMEM)] + [whole()] * 6,
        out_specs=(whole(), whole()),
        scratch_shapes=[
            pltpu.VMEM((groups, round_up(span + PAGE - 1, LANES)), f32),
            pltpu.VMEM((n_blk, span_rows, width), bf16),
        ],
        compiler_params=limit(8),
        name="span",
    )(page_owner.reshape(n_blk), own_stack, peer_stack, own_head, peer_head, inputs, bias)

    mixed = pl.pallas_call(
        finish_kernel,
        out_shape=jax.ShapeDtypeStruct((span_rows, width), bf16),
        in_specs=[whole()] * 3,
        out_specs=whole(),
        compiler_params=limit(8),
        name="finish",
    )(parts, span_gate[0], extra)
    return mixed[None], pool.reshape(1, MOST * PAGE, width)


def solution(mesh):
    return jax.shard_map(
        per_device,
        mesh=mesh,
        in_specs=(
            P("tenant", "blk", None),
            P("tenant", "blk", None),
            P("tenant", "blk", None),
            P("tenant", "blk", None),
            P(("blk", "tenant"), None),
            P(("blk", "tenant")),
            P("tenant"),
            P("tenant", None, None),
        ),
        out_specs=(P("tenant", "blk", None), P("tenant", "blk", None)),
        check_vma=False,
    )
```

```python
import functools

import jax
import jax.numpy as jnp
from jax import lax
from jax.experimental import pallas as pl
from jax.experimental.pallas import tpu as pltpu
from jax.sharding import PartitionSpec as P

PAGE = 8
MOST = 2
LANES = 128

bf16 = jnp.bfloat16
f32 = jnp.float32


def round_up(value, step):
    return -(-value // step) * step


def middle_out(count):
    low, high = list(range(count // 2))[::-1], list(range(count // 2, count))
    return [chip for pair in zip(low, high, strict=True) for chip in pair]


def part_order(n_blk):
    return [2 * chip + core for chip in middle_out(n_blk // 2) for core in (1, 0)]


def tap_order(n_blk, n_ten):
    chips = middle_out(n_blk // 2)
    chips = chips[len(chips) // 2 :] + chips[: len(chips) // 2]
    return [
        (2 * chip + core) * n_ten + tenant
        for core in range(2)
        for chip in chips
        for tenant in range(n_ten)
    ]


def tap_place(number, n_blk, n_ten):
    order = tap_order(n_blk, n_ten)
    block, tenant = lax.div(number, n_ten), lax.rem(number, n_ten)
    core, chip = lax.rem(block, 2), lax.div(block, 2)
    place = jnp.int32(0)
    for each in range(n_blk // 2):
        place = jnp.where(chip == each, order.index(2 * each * n_ten), place)
    return place + core * (len(order) // 2) + tenant


def pack_kernel(order, n_ten, taps_hbm, bias_hbm, key_hbm, value_hbm, send_ref, input_ref, *scratch):
    held, sems = scratch[:-1], scratch[-1]
    copies = [
        pltpu.make_async_copy(source, target, sems.at[i])
        for i, (source, target) in enumerate(
            zip((taps_hbm, bias_hbm, key_hbm, value_hbm), held, strict=True)
        )
    ]
    for copy in copies:
        copy.start()
    for copy in copies:
        copy.wait()
    taps_ref, bias_ref, key_ref, value_ref = held
    n_dev, padded, lanes = send_ref.shape
    rows = taps_ref.shape[0]
    bias = bias_ref[...].astype(f32)
    if bias.shape[1] < lanes:
        bias = jnp.concatenate([bias, jnp.zeros((1, lanes - bias.shape[1]), f32)], axis=1)
    blocks = []
    for half in range(2):
        taps = taps_ref[:, half * lanes : (half + 1) * lanes].astype(f32)
        parts = [taps, bias]
        if padded > rows + 1:
            parts.append(jnp.zeros((padded - rows - 1, lanes), f32))
        blocks.append(jnp.concatenate(parts, axis=0).astype(bf16))
    for place in range(n_dev):
        send_ref[place] = blocks[(order[place] // n_ten) % 2]
    input_ref[...] = (key_ref[...].astype(f32) * value_ref[...].astype(f32)).astype(bf16)


def source_kernel(len_ref, own_ref, peer_ref, out_ref):
    blk = lax.axis_index("blk")
    core = lax.rem(blk, 2)
    rows, width = own_ref.shape
    start = (blk - core) * rows
    length = len_ref[0]

    def masked(value, first):
        index = first + lax.broadcasted_iota(jnp.int32, (rows, width), 0)
        return jnp.where(index < length, value.astype(f32), 0.0).astype(bf16)

    own_at = pl.multiple_of(core * rows, rows)
    peer_at = pl.multiple_of((1 - core) * rows, rows)
    out_ref[pl.ds(own_at, rows), :] = masked(own_ref[...], start + core * rows)
    out_ref[pl.ds(peer_at, rows), :] = masked(peer_ref[...], start + (1 - core) * rows)


def reversed_taps(window, first, fr, top_lag, lanes):
    blocks, padded, groups = window.shape
    shape = (blocks, padded, lanes)
    block = lax.broadcasted_iota(jnp.int32, shape, 0)
    row = lax.broadcasted_iota(jnp.int32, shape, 1)
    lane = lax.broadcasted_iota(jnp.int32, shape, 2)
    lag = (first + block) * fr + row
    pick = jnp.where((row < fr) & (lag + lane == top_lag), 1.0, 0.0)
    pick = pick.reshape(blocks * padded, lanes).astype(bf16)
    return lax.dot_general(
        window.reshape(blocks * padded, groups),
        pick,
        (((0,), (0,)), ((), ())),
        preferred_element_type=f32,
    )


def toeplitz_product(taps_ref, first_group, gsize, outputs, depth, source):
    per = LANES // gsize
    lanes = taps_ref.shape[1]
    tiles = []
    for g in range(per):
        line = jnp.broadcast_to(taps_ref[pl.ds(first_group + g, 1), :], (outputs, lanes))
        line = pltpu.roll(line, lanes - (outputs - 1), 1, stride=1, stride_axis=0)
        tiles.append(line[:, :depth])
    matrix = jnp.concatenate(tiles, axis=0).astype(bf16)
    product = jnp.dot(matrix, source, preferred_element_type=f32)
    group = lax.broadcasted_iota(jnp.int32, (outputs, LANES), 1) // gsize
    total = product[:outputs]
    for g in range(1, per):
        total = jnp.where(group == g, product[g * outputs : (g + 1) * outputs], total)
    return total


def conv_kernel(fr, n_ten, gsize, len_ref, taps_ref, source_ref, out_ref, line_ref):
    n_dev, _, groups = taps_ref.shape
    n_blk, page, _ = out_ref.shape
    span = n_blk * page
    rows = source_ref.shape[0]
    base = len_ref[0] - lax.div(lax.axis_index("blk"), 2) * rows
    blocks = min(n_dev, -(-(fr - 1 + rows + span - 1) // fr))
    low = jnp.maximum(base - rows + 1, 0)
    first = jnp.clip(lax.div(low, fr), 0, n_dev - blocks)
    window = [taps_ref[tap_place(first + i, n_blk, n_ten)] for i in range(blocks)]
    line_ref[...] = reversed_taps(
        jnp.stack(window), first, fr, base + span - 1, line_ref.shape[1]
    )
    per = LANES // gsize
    for index in range(groups // per):
        columns = slice(index * LANES, (index + 1) * LANES)
        total = toeplitz_product(
            line_ref, index * per, gsize, span, rows, source_ref[:, columns]
        )
        for place, block in enumerate(part_order(n_blk)):
            out_ref[place, :, columns] = total[block * page : (block + 1) * page].astype(bf16)


def gather_kernel(order, fr, bias_width, _, taps_ref, *refs):
    pages, (stack_ref, head_ref, bias_ref) = refs[:-3], refs[-3:]
    chip = lax.div(lax.axis_index("blk"), 2)
    for step, page in enumerate(pages):
        stack_ref[lax.bitwise_xor(chip, step)] = page[...]
    for index in range(head_ref.shape[0]):
        head_ref[index] = taps_ref[order.index(index)]
    each = LANES // bias_width
    for index in range(taps_ref.shape[0] // each):
        row = [
            taps_ref[order.index(index * each + i), fr : fr + 1, :bias_width].astype(f32)
            for i in range(each)
        ]
        row = row[0] if each == 1 else jnp.concatenate(row, axis=1)
        bias_ref[:, index * LANES : (index + 1) * LANES] = row


def span_kernel(
    fr,
    gsize,
    owner_ref,
    own_stack_ref,
    peer_stack_ref,
    own_head_ref,
    peer_head_ref,
    input_ref,
    bias_ref,
    extra_ref,
    pool_ref,
    line_ref,
    source_ref,
):
    blk = lax.axis_index("blk")
    core = lax.rem(blk, 2)
    n_chip, page, width = own_stack_ref.shape
    n_blk = 2 * n_chip
    pool_ref[...] = jnp.zeros_like(pool_ref)
    for chip in range(n_chip):
        for stack, side in ((own_stack_ref, core), (peer_stack_ref, 1 - core)):
            number = 2 * chip + side
            value = stack[chip]
            source_ref[number] = value
            owner = owner_ref[number]
            rank = jnp.int32(0)
            for other in range(n_blk):
                earlier = (owner_ref[other] == owner) & (other < number)
                rank = rank + earlier.astype(jnp.int32)

            @pl.when(owner == blk)
            def _(value=value, rank=rank):
                pool_ref[rank] = value

    groups = own_head_ref.shape[2]
    lanes = line_ref.shape[1]
    top_lag = blk * page + page - 1
    for head, side in ((own_head_ref, core), (peer_head_ref, 1 - core)):
        at = pl.multiple_of(side * groups, groups)
        line_ref[pl.ds(at, groups), :] = reversed_taps(head[...], 0, fr, top_lag, lanes)
    per = LANES // gsize
    for index in range(width // LANES):
        columns = slice(index * LANES, (index + 1) * LANES)
        source = source_ref[:, :, columns].reshape(n_blk * page, LANES)
        total = toeplitz_product(line_ref, index * per, gsize, page, n_blk * page, source)
        skip = bias_ref[:, columns] * input_ref[:, columns].astype(f32)
        extra_ref[:, columns] = total + skip


def finish_kernel(parts_ref, gate_ref, extra_ref, mixed_ref):
    n_blk, _, half = parts_ref.shape
    for core in range(2):
        columns = slice(core * half, (core + 1) * half)
        total = extra_ref[:, columns]
        for place, block in enumerate(part_order(n_blk)):
            if block % 2 == core:
                total = total + parts_ref[place].astype(f32)
        gate = gate_ref[:, columns].astype(f32)
        mixed_ref[:, columns] = (gate * total).astype(bf16)


def whole(memory=pltpu.VMEM):
    return pl.BlockSpec(memory_space=memory)


def limit(mebibytes):
    return pltpu.CompilerParams(vmem_limit_bytes=mebibytes << 20)


def per_device(
    history_u, span_gate, span_key, span_value, filter_taps, skip_bias, lengths, page_owner
):
    n_blk, n_ten = lax.axis_size("blk"), lax.axis_size("tenant")
    n_dev, n_chip = n_blk * n_ten, n_blk // 2
    history = history_u[0]
    rows, width = history.shape
    half = width // 2
    span_rows = span_key.shape[1]
    span = span_rows * n_blk
    fr, groups = filter_taps.shape
    gsize = width // groups
    padded = round_up(fr + 1, 8)
    bias_width = skip_bias.shape[0]
    swap = [(i, i ^ 1) for i in range(n_blk)]

    send, inputs = pl.pallas_call(
        functools.partial(pack_kernel, tap_order(n_blk, n_ten), n_ten),
        out_shape=(
            jax.ShapeDtypeStruct((n_dev, padded, groups // 2), bf16),
            jax.ShapeDtypeStruct((span_rows, width), bf16),
        ),
        in_specs=[whole(pltpu.HBM)] * 4,
        out_specs=(whole(), whole()),
        scratch_shapes=[
            pltpu.VMEM((fr, groups), bf16),
            pltpu.VMEM((1, bias_width), bf16),
            pltpu.VMEM((span_rows, width), bf16),
            pltpu.VMEM((span_rows, width), bf16),
            pltpu.SemaphoreType.DMA((4,)),
        ],
        compiler_params=limit(58),
        name="pack",
    )(filter_taps, skip_bias.reshape(1, bias_width), span_key[0], span_value[0])

    taps = lax.all_to_all(
        send,
        ("blk", "tenant"),
        split_axis=0,
        concat_axis=0,
        axis_index_groups=[tap_order(n_blk, n_ten)],
        tiled=True,
    )
    peer_history = lax.ppermute(history, "blk", swap)

    def half_block(count):
        return pl.BlockSpec((count, half), lambda i, n: (0, lax.rem(lax.axis_index("blk"), 2)))

    source = pl.pallas_call(
        source_kernel,
        grid_spec=pltpu.PrefetchScalarGridSpec(
            num_scalar_prefetch=1,
            grid=(1,),
            in_specs=[half_block(rows), half_block(rows)],
            out_specs=pl.BlockSpec((2 * rows, half), lambda i, n: (0, 0)),
        ),
        out_shape=jax.ShapeDtypeStruct((2 * rows, half), bf16),
        compiler_params=limit(8),
        name="source",
    )(lengths, history, peer_history)

    pages = {0: inputs}
    far = n_chip // 2
    while far:
        across = [(i, i ^ (2 * far)) for i in range(n_blk)]
        pages.update({at ^ far: lax.ppermute(page, "blk", across) for at, page in pages.items()})
        far //= 2
    pages = [pages[at] for at in range(n_chip)]

    partial = pl.pallas_call(
        functools.partial(conv_kernel, fr, n_ten, gsize),
        out_shape=jax.ShapeDtypeStruct((n_blk, span_rows, half), bf16),
        in_specs=[whole(pltpu.SMEM), whole(), whole()],
        out_specs=whole(),
        scratch_shapes=[pltpu.VMEM((groups // 2, round_up(2 * rows + span - 1, LANES)), f32)],
        compiler_params=limit(16),
        name="conv",
    )(lengths, taps, source)

    partial, *pages = lax.optimization_barrier((partial, *pages))
    parts = lax.all_to_all(
        partial,
        "blk",
        split_axis=0,
        concat_axis=0,
        axis_index_groups=[part_order(n_blk)],
        tiled=True,
    )

    stack = jax.ShapeDtypeStruct((n_chip, span_rows, width), bf16)
    head = jax.ShapeDtypeStruct((min(n_dev, -(-span // fr)), padded, groups // 2), bf16)
    own_stack, own_head, bias = pl.pallas_call(
        functools.partial(gather_kernel, tap_order(n_blk, n_ten), fr, bias_width),
        out_shape=(stack, head, jax.ShapeDtypeStruct((1, width), f32)),
        in_specs=[whole(pl.ANY)] + [whole()] * (1 + n_chip),
        out_specs=(whole(),) * 3,
        compiler_params=limit(8),
        name="gather",
    )(partial, taps, *pages)
    peer_stack = lax.ppermute(own_stack, "blk", swap)
    peer_head = lax.ppermute(own_head, "blk", swap)

    extra, pool = pl.pallas_call(
        functools.partial(span_kernel, fr, gsize),
        out_shape=(
            jax.ShapeDtypeStruct((span_rows, width), f32),
            jax.ShapeDtypeStruct((MOST, PAGE, width), bf16),
        ),
        in_specs=[whole(pltpu.SMEM)] + [whole()] * 6,
        out_specs=(whole(), whole()),
        scratch_shapes=[
            pltpu.VMEM((groups, round_up(span + PAGE - 1, LANES)), f32),
            pltpu.VMEM((n_blk, span_rows, width), bf16),
        ],
        compiler_params=limit(8),
        name="span",
    )(page_owner.reshape(n_blk), own_stack, peer_stack, own_head, peer_head, inputs, bias)

    mixed = pl.pallas_call(
        finish_kernel,
        out_shape=jax.ShapeDtypeStruct((span_rows, width), bf16),
        in_specs=[whole()] * 3,
        out_specs=whole(),
        compiler_params=limit(8),
        name="finish",
    )(parts, span_gate[0], extra)
    return mixed[None], pool.reshape(1, MOST * PAGE, width)


def solution(mesh):
    return jax.shard_map(
        per_device,
        mesh=mesh,
        in_specs=(
            P("tenant", "blk", None),
            P("tenant", "blk", None),
            P("tenant", "blk", None),
            P("tenant", "blk", None),
            P(("blk", "tenant"), None),
            P(("blk", "tenant")),
            P("tenant"),
            P("tenant", None, None),
        ),
        out_specs=(P("tenant", "blk", None), P("tenant", "blk", None)),
        check_vma=False,
    )
```

```python
import functools

import jax
import jax.numpy as jnp
from jax import lax
from jax.experimental import pallas as pl
from jax.experimental.pallas import tpu as pltpu
from jax.sharding import PartitionSpec as P

PAGE = 8
MOST = 2
LANES = 128

bf16 = jnp.bfloat16
f32 = jnp.float32


def round_up(value, step):
    return -(-value // step) * step


def middle_out(count):
    low, high = list(range(count // 2))[::-1], list(range(count // 2, count))
    return [chip for pair in zip(low, high, strict=True) for chip in pair]


def part_order(n_blk):
    return [2 * chip + core for chip in middle_out(n_blk // 2) for core in (1, 0)]


def tap_order(n_blk, n_ten):
    chips = middle_out(n_blk // 2)
    chips = chips[len(chips) // 2 :] + chips[: len(chips) // 2]
    return [
        (2 * chip + core) * n_ten + tenant
        for core in range(2)
        for chip in chips
        for tenant in range(n_ten)
    ]


def tap_place(number, n_blk, n_ten):
    order = tap_order(n_blk, n_ten)
    block, tenant = lax.div(number, n_ten), lax.rem(number, n_ten)
    core, chip = lax.rem(block, 2), lax.div(block, 2)
    place = jnp.int32(0)
    for each in range(n_blk // 2):
        place = jnp.where(chip == each, order.index(2 * each * n_ten), place)
    return place + core * (len(order) // 2) + tenant


def pack_kernel(order, n_ten, taps_hbm, bias_hbm, send_ref, token_ref, *scratch):
    held, sems = scratch[:-1], scratch[-1]
    copies = [
        pltpu.make_async_copy(source, target, sems.at[i])
        for i, (source, target) in enumerate(zip((taps_hbm, bias_hbm), held, strict=True))
    ]
    for copy in copies:
        copy.start()
    token_ref[...] = jnp.zeros_like(token_ref)
    for copy in copies:
        copy.wait()
    taps_ref, bias_ref = held
    n_dev, pairs, _, lanes = send_ref.shape
    padded = 2 * pairs
    rows = taps_ref.shape[0]
    bias = bias_ref[...].astype(f32)
    if bias.shape[1] < lanes:
        bias = jnp.concatenate([bias, jnp.zeros((1, lanes - bias.shape[1]), f32)], axis=1)
    blocks = []
    for half in range(2):
        taps = taps_ref[:, half * lanes : (half + 1) * lanes].astype(f32)
        parts = [taps, bias]
        if padded > rows + 1:
            parts.append(jnp.zeros((padded - rows - 1, lanes), f32))
        blocks.append(jnp.concatenate(parts, axis=0).astype(bf16).reshape(pairs, 2, lanes))
    for place in range(n_dev):
        send_ref[place] = blocks[(order[place] // n_ten) % 2]


def input_kernel(_, key_ref, value_ref, input_ref):
    input_ref[...] = (key_ref[...].astype(f32) * value_ref[...].astype(f32)).astype(bf16)


def source_kernel(len_ref, own_ref, peer_ref, out_ref):
    blk = lax.axis_index("blk")
    core = lax.rem(blk, 2)
    rows, width = own_ref.shape
    start = (blk - core) * rows
    length = len_ref[0]

    def masked(value, first):
        index = first + lax.broadcasted_iota(jnp.int32, (rows, width), 0)
        return jnp.where(index < length, value.astype(f32), 0.0).astype(bf16)

    own_at = pl.multiple_of(core * rows, rows)
    peer_at = pl.multiple_of((1 - core) * rows, rows)
    out_ref[pl.ds(own_at, rows), :] = masked(own_ref[...], start + core * rows)
    out_ref[pl.ds(peer_at, rows), :] = masked(peer_ref[...], start + (1 - core) * rows)


def reversed_taps(window, first, fr, top_lag, lanes):
    blocks, padded, groups = window.shape
    shape = (blocks * padded, lanes)
    index = lax.broadcasted_iota(jnp.int32, shape, 0)
    lane = lax.broadcasted_iota(jnp.int32, shape, 1)
    block = lax.div(index * ((1 << 16) // padded + 1), 1 << 16)
    row = index - block * padded
    lag = (first + block) * fr + row
    pick = jnp.where((row < fr) & (lag + lane == top_lag), 1.0, 0.0).astype(bf16)
    return lax.dot_general(
        window.reshape(blocks * padded, groups),
        pick,
        (((0,), (0,)), ((), ())),
        preferred_element_type=f32,
    )


def toeplitz_product(taps_ref, first_group, gsize, outputs, depth, source):
    per = LANES // gsize
    lanes = taps_ref.shape[1]
    tiles = []
    for g in range(per):
        line = jnp.broadcast_to(taps_ref[pl.ds(first_group + g, 1), :], (outputs, lanes))
        line = pltpu.roll(line, lanes - (outputs - 1), 1, stride=1, stride_axis=0)
        tiles.append(line[:, :depth])
    matrix = jnp.concatenate(tiles, axis=0).astype(bf16)
    product = jnp.dot(matrix, source, preferred_element_type=f32)
    group = lax.broadcasted_iota(jnp.int32, (outputs, LANES), 1) // gsize
    total = product[:outputs]
    for g in range(1, per):
        total = jnp.where(group == g, product[g * outputs : (g + 1) * outputs], total)
    return total


def conv_kernel(fr, n_ten, gsize, len_ref, taps_ref, source_ref, out_ref, line_ref):
    n_dev, pairs, _, groups = taps_ref.shape
    n_blk, page, _ = out_ref.shape
    span = n_blk * page
    rows = source_ref.shape[0]
    base = len_ref[0] - lax.div(lax.axis_index("blk"), 2) * rows
    blocks = min(n_dev, -(-(fr - 1 + rows + span - 1) // fr))
    low = jnp.maximum(base - rows + 1, 0)
    first = jnp.clip(lax.div(low, fr), 0, n_dev - blocks)
    window = [
        taps_ref[tap_place(first + i, n_blk, n_ten)].reshape(2 * pairs, groups)
        for i in range(blocks)
    ]
    line_ref[...] = reversed_taps(
        jnp.stack(window), first, fr, base + span - 1, line_ref.shape[1]
    )
    per = LANES // gsize
    for index in range(groups // per):
        columns = slice(index * LANES, (index + 1) * LANES)
        total = toeplitz_product(
            line_ref, index * per, gsize, span, rows, source_ref[:, columns]
        )
        for place, block in enumerate(part_order(n_blk)):
            out_ref[place, :, columns] = total[block * page : (block + 1) * page].astype(bf16)


def gather_kernel(order, fr, bias_width, _, taps_ref, *refs):
    pages, (stack_ref, head_ref, bias_ref) = refs[:-3], refs[-3:]
    chip = lax.div(lax.axis_index("blk"), 2)
    n_chip = len(pages)
    for step, page in enumerate(pages):
        stack_ref[lax.rem(chip + n_chip - step, n_chip)] = page[...]
    for index in range(head_ref.shape[0]):
        head_ref[index] = taps_ref[order.index(index)].reshape(head_ref.shape[1:])
    each = LANES // bias_width
    for index in range(taps_ref.shape[0] // each):
        row = [
            taps_ref[order.index(index * each + i), fr // 2, fr % 2 : fr % 2 + 1, :bias_width].astype(f32)
            for i in range(each)
        ]
        row = row[0] if each == 1 else jnp.concatenate(row, axis=1)
        bias_ref[:, index * LANES : (index + 1) * LANES] = row


def span_kernel(
    fr,
    gsize,
    owner_ref,
    own_stack_ref,
    peer_stack_ref,
    own_head_ref,
    peer_head_ref,
    input_ref,
    bias_ref,
    extra_ref,
    pool_ref,
    line_ref,
    source_ref,
):
    blk = lax.axis_index("blk")
    core = lax.rem(blk, 2)
    n_chip, page, width = own_stack_ref.shape
    n_blk = 2 * n_chip
    pool_ref[...] = jnp.zeros_like(pool_ref)
    for chip in range(n_chip):
        for stack, side in ((own_stack_ref, core), (peer_stack_ref, 1 - core)):
            number = 2 * chip + side
            value = stack[chip]
            source_ref[number] = value
            owner = owner_ref[number]
            rank = jnp.int32(0)
            for other in range(n_blk):
                earlier = (owner_ref[other] == owner) & (other < number)
                rank = rank + earlier.astype(jnp.int32)

            @pl.when(owner == blk)
            def _(value=value, rank=rank):
                pool_ref[rank] = value

    groups = own_head_ref.shape[2]
    lanes = line_ref.shape[1]
    top_lag = blk * page + page - 1
    for head, side in ((own_head_ref, core), (peer_head_ref, 1 - core)):
        at = pl.multiple_of(side * groups, groups)
        line_ref[pl.ds(at, groups), :] = reversed_taps(head[...], 0, fr, top_lag, lanes)
    per = LANES // gsize
    for index in range(width // LANES):
        columns = slice(index * LANES, (index + 1) * LANES)
        source = source_ref[:, :, columns].reshape(n_blk * page, LANES)
        total = toeplitz_product(line_ref, index * per, gsize, page, n_blk * page, source)
        skip = bias_ref[:, columns] * input_ref[:, columns].astype(f32)
        extra_ref[:, columns] = total + skip


def finish_kernel(parts_ref, gate_ref, extra_ref, mixed_ref):
    n_blk, _, half = parts_ref.shape
    for core in range(2):
        columns = slice(core * half, (core + 1) * half)
        total = extra_ref[:, columns]
        for place, block in enumerate(part_order(n_blk)):
            if block % 2 == core:
                total = total + parts_ref[place].astype(f32)
        gate = gate_ref[:, columns].astype(f32)
        mixed_ref[:, columns] = (gate * total).astype(bf16)


def whole(memory=pltpu.VMEM):
    return pl.BlockSpec(memory_space=memory)


def limit(mebibytes):
    return pltpu.CompilerParams(vmem_limit_bytes=mebibytes << 20)


def per_device(
    history_u, span_gate, span_key, span_value, filter_taps, skip_bias, lengths, page_owner
):
    n_blk, n_ten = lax.axis_size("blk"), lax.axis_size("tenant")
    n_dev, n_chip = n_blk * n_ten, n_blk // 2
    history = history_u[0]
    rows, width = history.shape
    half = width // 2
    span_rows = span_key.shape[1]
    span = span_rows * n_blk
    fr, groups = filter_taps.shape
    gsize = width // groups
    pairs = round_up(fr + 1, 2) // 2
    bias_width = skip_bias.shape[0]
    swap = [(i, i ^ 1) for i in range(n_blk)]

    send, token = pl.pallas_call(
        functools.partial(pack_kernel, tap_order(n_blk, n_ten), n_ten),
        out_shape=(
            jax.ShapeDtypeStruct((n_dev, pairs, 2, groups // 2), bf16),
            jax.ShapeDtypeStruct((8, LANES), f32),
        ),
        in_specs=[whole(pltpu.HBM)] * 2,
        out_specs=(whole(), whole()),
        scratch_shapes=[
            pltpu.VMEM((fr, groups), bf16),
            pltpu.VMEM((1, bias_width), bf16),
            pltpu.SemaphoreType.DMA((2,)),
        ],
        compiler_params=limit(58),
        name="pack",
    )(filter_taps, skip_bias.reshape(1, bias_width))
    taps = lax.all_to_all(
        send,
        ("blk", "tenant"),
        split_axis=0,
        concat_axis=0,
        axis_index_groups=[tap_order(n_blk, n_ten)],
        tiled=True,
    )
    peer_history = lax.ppermute(history, "blk", swap)

    def half_block(count):
        return pl.BlockSpec((count, half), lambda i, n: (0, lax.rem(lax.axis_index("blk"), 2)))

    source = pl.pallas_call(
        source_kernel,
        grid_spec=pltpu.PrefetchScalarGridSpec(
            num_scalar_prefetch=1,
            grid=(1,),
            in_specs=[half_block(rows), half_block(rows)],
            out_specs=pl.BlockSpec((2 * rows, half), lambda i, n: (0, 0)),
        ),
        out_shape=jax.ShapeDtypeStruct((2 * rows, half), bf16),
        compiler_params=limit(8),
        name="source",
    )(lengths, history, peer_history)

    inputs = pl.pallas_call(
        input_kernel,
        out_shape=jax.ShapeDtypeStruct((span_rows, width), bf16),
        in_specs=[whole(pl.ANY)] + [whole()] * 2,
        out_specs=whole(),
        compiler_params=limit(8),
        cost_estimate=pl.CostEstimate(flops=32768, bytes_accessed=3 * span_rows * width * 2, transcendentals=0),
        name="inputs",
    )(source, span_key[0], span_value[0])

    pages = [inputs]
    for step in range(1, n_chip):
        turn = [(i, (i + 2 * step) % n_blk) for i in range(n_blk)]
        pages.append(lax.ppermute(inputs, "blk", turn))
    partial = pl.pallas_call(
        functools.partial(conv_kernel, fr, n_ten, gsize),
        out_shape=jax.ShapeDtypeStruct((n_blk, span_rows, half), bf16),
        in_specs=[whole(pltpu.SMEM), whole(), whole()],
        out_specs=whole(),
        scratch_shapes=[pltpu.VMEM((groups // 2, round_up(2 * rows + span - 1, LANES)), f32)],
        compiler_params=limit(16),
        name="conv",
    )(lengths, taps, source)

    partial, *pages = lax.optimization_barrier((partial, *pages))
    parts = lax.all_to_all(
        partial,
        "blk",
        split_axis=0,
        concat_axis=0,
        axis_index_groups=[part_order(n_blk)],
        tiled=True,
    )

    stack = jax.ShapeDtypeStruct((n_chip, span_rows, width), bf16)
    head = jax.ShapeDtypeStruct((min(n_dev, -(-span // fr)), 2 * pairs, groups // 2), bf16)
    own_stack, own_head, bias = pl.pallas_call(
        functools.partial(gather_kernel, tap_order(n_blk, n_ten), fr, bias_width),
        out_shape=(stack, head, jax.ShapeDtypeStruct((1, width), f32)),
        in_specs=[whole(pl.ANY)] + [whole()] * (1 + n_chip),
        out_specs=(whole(),) * 3,
        compiler_params=limit(8),
        name="gather",
    )(partial, taps, *pages)
    peer_stack = lax.ppermute(own_stack, "blk", swap)
    peer_head = lax.ppermute(own_head, "blk", swap)

    extra, pool = pl.pallas_call(
        functools.partial(span_kernel, fr, gsize),
        out_shape=(
            jax.ShapeDtypeStruct((span_rows, width), f32),
            jax.ShapeDtypeStruct((MOST, PAGE, width), bf16),
        ),
        in_specs=[whole(pltpu.SMEM)] + [whole()] * 6,
        out_specs=(whole(), whole()),
        scratch_shapes=[
            pltpu.VMEM((groups, round_up(span + PAGE - 1, LANES)), f32),
            pltpu.VMEM((n_blk, span_rows, width), bf16),
        ],
        compiler_params=limit(8),
        name="span",
    )(page_owner.reshape(n_blk), own_stack, peer_stack, own_head, peer_head, inputs, bias)

    mixed = pl.pallas_call(
        finish_kernel,
        out_shape=jax.ShapeDtypeStruct((span_rows, width), bf16),
        in_specs=[whole()] * 3,
        out_specs=whole(),
        compiler_params=limit(8),
        name="finish",
    )(parts, span_gate[0], extra)
    return mixed[None], pool.reshape(1, MOST * PAGE, width)


def solution(mesh):
    return jax.shard_map(
        per_device,
        mesh=mesh,
        in_specs=(
            P("tenant", "blk", None),
            P("tenant", "blk", None),
            P("tenant", "blk", None),
            P("tenant", "blk", None),
            P(("blk", "tenant"), None),
            P(("blk", "tenant")),
            P("tenant"),
            P("tenant", None, None),
        ),
        out_specs=(P("tenant", "blk", None), P("tenant", "blk", None)),
        check_vma=False,
    )
```

```python
import functools

import jax
import jax.numpy as jnp
from jax import lax
from jax.experimental import pallas as pl
from jax.experimental.pallas import tpu as pltpu
from jax.sharding import PartitionSpec as P

PAGE = 8
MOST = 2
LANES = 128

bf16 = jnp.bfloat16
f32 = jnp.float32


def round_up(value, step):
    return -(-value // step) * step


def middle_out(count):
    low, high = list(range(count // 2))[::-1], list(range(count // 2, count))
    return [chip for pair in zip(low, high, strict=True) for chip in pair]


def part_order(n_blk):
    return [2 * chip + core for chip in middle_out(n_blk // 2) for core in (1, 0)]


def tap_order(n_blk, n_ten):
    chips = middle_out(n_blk // 2)
    chips = chips[len(chips) // 2 :] + chips[: len(chips) // 2]
    return [
        (2 * chip + core) * n_ten + tenant
        for core in range(2)
        for chip in chips
        for tenant in range(n_ten)
    ]


def tap_place(number, n_blk, n_ten):
    order = tap_order(n_blk, n_ten)
    block, tenant = lax.div(number, n_ten), lax.rem(number, n_ten)
    core, chip = lax.rem(block, 2), lax.div(block, 2)
    place = jnp.int32(0)
    for each in range(n_blk // 2):
        place = jnp.where(chip == each, order.index(2 * each * n_ten), place)
    return place + core * (len(order) // 2) + tenant


def pack_kernel(order, n_ten, taps_hbm, bias_hbm, send_ref, token_ref, *scratch):
    held, sems = scratch[:-1], scratch[-1]
    copies = [
        pltpu.make_async_copy(source, target, sems.at[i])
        for i, (source, target) in enumerate(zip((taps_hbm, bias_hbm), held, strict=True))
    ]
    for copy in copies:
        copy.start()
    token_ref[...] = jnp.zeros_like(token_ref)
    for copy in copies:
        copy.wait()
    taps_ref, bias_ref = held
    n_dev, pairs, _, lanes = send_ref.shape
    padded = 2 * pairs
    rows = taps_ref.shape[0]
    bias = bias_ref[...].astype(f32)
    if bias.shape[1] < lanes:
        bias = jnp.concatenate([bias, jnp.zeros((1, lanes - bias.shape[1]), f32)], axis=1)
    blocks = []
    for half in range(2):
        taps = taps_ref[:, half * lanes : (half + 1) * lanes].astype(f32)
        parts = [taps, bias]
        if padded > rows + 1:
            parts.append(jnp.zeros((padded - rows - 1, lanes), f32))
        blocks.append(jnp.concatenate(parts, axis=0).astype(bf16).reshape(pairs, 2, lanes))
    for place in range(n_dev):
        send_ref[place] = blocks[(order[place] // n_ten) % 2]


def input_kernel(_, key_ref, value_ref, input_ref):
    input_ref[...] = (key_ref[...].astype(f32) * value_ref[...].astype(f32)).astype(bf16)


def source_kernel(len_ref, own_ref, *refs):
    peer_refs, out_ref = refs[:-1], refs[-1]
    blk = lax.axis_index("blk")
    core = lax.rem(blk, 2)
    rows, width = own_ref.shape
    start = (blk - core) * rows
    length = len_ref[0]

    def masked(value, first):
        index = first + lax.broadcasted_iota(jnp.int32, value.shape, 0)
        return jnp.where(index < length, value.astype(f32), 0.0).astype(bf16)

    own_at = pl.multiple_of(core * rows, rows)
    out_ref[pl.ds(own_at, rows), :] = masked(own_ref[...], start + core * rows)
    piece = rows // len(peer_refs)
    for i, peer_ref in enumerate(peer_refs):
        peer_at = pl.multiple_of((1 - core) * rows + i * piece, piece)
        out_ref[pl.ds(peer_at, piece), :] = masked(peer_ref[...], start + peer_at)


def reversed_taps(window, first, fr, top_lag, lanes):
    blocks, padded, groups = window.shape
    shape = (blocks * padded, lanes)
    index = lax.broadcasted_iota(jnp.int32, shape, 0)
    lane = lax.broadcasted_iota(jnp.int32, shape, 1)
    block = lax.div(index * ((1 << 16) // padded + 1), 1 << 16)
    row = index - block * padded
    lag = (first + block) * fr + row
    pick = jnp.where((row < fr) & (lag + lane == top_lag), 1.0, 0.0).astype(bf16)
    return lax.dot_general(
        window.reshape(blocks * padded, groups),
        pick,
        (((0,), (0,)), ((), ())),
        preferred_element_type=f32,
    )


def toeplitz_product(taps_ref, first_group, gsize, outputs, depth, source):
    per = LANES // gsize
    lanes = taps_ref.shape[1]
    tiles = []
    for g in range(per):
        line = jnp.broadcast_to(taps_ref[pl.ds(first_group + g, 1), :], (outputs, lanes))
        line = pltpu.roll(line, lanes - (outputs - 1), 1, stride=1, stride_axis=0)
        tiles.append(line[:, :depth])
    matrix = jnp.concatenate(tiles, axis=0).astype(bf16)
    product = jnp.dot(matrix, source, preferred_element_type=f32)
    group = lax.broadcasted_iota(jnp.int32, (outputs, LANES), 1) // gsize
    total = product[:outputs]
    for g in range(1, per):
        total = jnp.where(group == g, product[g * outputs : (g + 1) * outputs], total)
    return total


def conv_kernel(fr, n_ten, gsize, len_ref, taps_ref, source_ref, out_ref, line_ref):
    n_dev, pairs, _, groups = taps_ref.shape
    n_blk, page, _ = out_ref.shape
    span = n_blk * page
    rows = source_ref.shape[0]
    base = len_ref[0] - lax.div(lax.axis_index("blk"), 2) * rows
    blocks = min(n_dev, -(-(fr - 1 + rows + span - 1) // fr))
    low = jnp.maximum(base - rows + 1, 0)
    first = jnp.clip(lax.div(low, fr), 0, n_dev - blocks)
    window = [
        taps_ref[tap_place(first + i, n_blk, n_ten)].reshape(2 * pairs, groups)
        for i in range(blocks)
    ]
    line_ref[...] = reversed_taps(
        jnp.stack(window), first, fr, base + span - 1, line_ref.shape[1]
    )
    per = LANES // gsize
    for index in range(groups // per):
        columns = slice(index * LANES, (index + 1) * LANES)
        total = toeplitz_product(
            line_ref, index * per, gsize, span, rows, source_ref[:, columns]
        )
        for place, block in enumerate(part_order(n_blk)):
            out_ref[place, :, columns] = total[block * page : (block + 1) * page].astype(bf16)


def gather_kernel(order, fr, bias_width, _, taps_ref, *refs):
    pages, (stack_ref, head_ref, bias_ref) = refs[:-3], refs[-3:]
    chip = lax.div(lax.axis_index("blk"), 2)
    n_chip = len(pages)
    for step, page in enumerate(pages):
        stack_ref[lax.rem(chip + n_chip - step, n_chip)] = page[...]
    for index in range(head_ref.shape[0]):
        head_ref[index] = taps_ref[order.index(index)].reshape(head_ref.shape[1:])
    each = LANES // bias_width
    for index in range(taps_ref.shape[0] // each):
        row = [
            taps_ref[order.index(index * each + i), fr // 2, fr % 2 : fr % 2 + 1, :bias_width].astype(f32)
            for i in range(each)
        ]
        row = row[0] if each == 1 else jnp.concatenate(row, axis=1)
        bias_ref[:, index * LANES : (index + 1) * LANES] = row


def span_kernel(
    fr,
    gsize,
    owner_ref,
    own_stack_ref,
    peer_stack_ref,
    own_head_ref,
    peer_head_ref,
    input_ref,
    bias_ref,
    extra_ref,
    pool_ref,
    line_ref,
    source_ref,
):
    blk = lax.axis_index("blk")
    core = lax.rem(blk, 2)
    n_chip, page, width = own_stack_ref.shape
    n_blk = 2 * n_chip
    pool_ref[...] = jnp.zeros_like(pool_ref)
    for chip in range(n_chip):
        for stack, side in ((own_stack_ref, core), (peer_stack_ref, 1 - core)):
            number = 2 * chip + side
            value = stack[chip]
            source_ref[number] = value
            owner = owner_ref[number]
            rank = jnp.int32(0)
            for other in range(n_blk):
                earlier = (owner_ref[other] == owner) & (other < number)
                rank = rank + earlier.astype(jnp.int32)

            @pl.when(owner == blk)
            def _(value=value, rank=rank):
                pool_ref[rank] = value

    groups = own_head_ref.shape[2]
    lanes = line_ref.shape[1]
    top_lag = blk * page + page - 1
    for head, side in ((own_head_ref, core), (peer_head_ref, 1 - core)):
        at = pl.multiple_of(side * groups, groups)
        line_ref[pl.ds(at, groups), :] = reversed_taps(head[...], 0, fr, top_lag, lanes)
    per = LANES // gsize
    for index in range(width // LANES):
        columns = slice(index * LANES, (index + 1) * LANES)
        source = source_ref[:, :, columns].reshape(n_blk * page, LANES)
        total = toeplitz_product(line_ref, index * per, gsize, page, n_blk * page, source)
        skip = bias_ref[:, columns] * input_ref[:, columns].astype(f32)
        extra_ref[:, columns] = total + skip


def finish_kernel(parts_ref, gate_ref, extra_ref, mixed_ref):
    n_blk, _, half = parts_ref.shape
    for core in range(2):
        columns = slice(core * half, (core + 1) * half)
        total = extra_ref[:, columns]
        for place, block in enumerate(part_order(n_blk)):
            if block % 2 == core:
                total = total + parts_ref[place].astype(f32)
        gate = gate_ref[:, columns].astype(f32)
        mixed_ref[:, columns] = (gate * total).astype(bf16)


def whole(memory=pltpu.VMEM):
    return pl.BlockSpec(memory_space=memory)


def limit(mebibytes):
    return pltpu.CompilerParams(vmem_limit_bytes=mebibytes << 20)


def per_device(
    history_u, span_gate, span_key, span_value, filter_taps, skip_bias, lengths, page_owner
):
    n_blk, n_ten = lax.axis_size("blk"), lax.axis_size("tenant")
    n_dev, n_chip = n_blk * n_ten, n_blk // 2
    history = history_u[0]
    rows, width = history.shape
    half = width // 2
    span_rows = span_key.shape[1]
    span = span_rows * n_blk
    fr, groups = filter_taps.shape
    gsize = width // groups
    pairs = round_up(fr + 1, 2) // 2
    bias_width = skip_bias.shape[0]
    swap = [(i, i ^ 1) for i in range(n_blk)]

    send, token = pl.pallas_call(
        functools.partial(pack_kernel, tap_order(n_blk, n_ten), n_ten),
        out_shape=(
            jax.ShapeDtypeStruct((n_dev, pairs, 2, groups // 2), bf16),
            jax.ShapeDtypeStruct((8, LANES), f32),
        ),
        in_specs=[whole(pltpu.HBM)] * 2,
        out_specs=(whole(), whole()),
        scratch_shapes=[
            pltpu.VMEM((fr, groups), bf16),
            pltpu.VMEM((1, bias_width), bf16),
            pltpu.SemaphoreType.DMA((2,)),
        ],
        compiler_params=limit(58),
        name="pack",
    )(filter_taps, skip_bias.reshape(1, bias_width))
    taps = lax.all_to_all(
        send,
        ("blk", "tenant"),
        split_axis=0,
        concat_axis=0,
        axis_index_groups=[tap_order(n_blk, n_ten)],
        tiled=True,
    )
    pieces = 4
    piece = rows // pieces
    peer_history = [
        lax.ppermute(history[i * piece : (i + 1) * piece], "blk", swap) for i in range(pieces)
    ]

    def half_block(count):
        return pl.BlockSpec((count, half), lambda i, n: (0, lax.rem(lax.axis_index("blk"), 2)))

    source = pl.pallas_call(
        source_kernel,
        grid_spec=pltpu.PrefetchScalarGridSpec(
            num_scalar_prefetch=1,
            grid=(1,),
            in_specs=[half_block(rows)] + [half_block(piece)] * pieces,
            out_specs=pl.BlockSpec((2 * rows, half), lambda i, n: (0, 0)),
        ),
        out_shape=jax.ShapeDtypeStruct((2 * rows, half), bf16),
        compiler_params=limit(8),
        name="source",
    )(lengths, history, *peer_history)

    inputs = pl.pallas_call(
        input_kernel,
        out_shape=jax.ShapeDtypeStruct((span_rows, width), bf16),
        in_specs=[whole(pl.ANY)] + [whole()] * 2,
        out_specs=whole(),
        compiler_params=limit(8),
        cost_estimate=pl.CostEstimate(flops=32768, bytes_accessed=3 * span_rows * width * 2, transcendentals=0),
        name="inputs",
    )(source, span_key[0], span_value[0])

    pages = [inputs]
    for step in range(1, n_chip):
        turn = [(i, (i + 2 * step) % n_blk) for i in range(n_blk)]
        pages.append(lax.ppermute(inputs, "blk", turn))
    partial = pl.pallas_call(
        functools.partial(conv_kernel, fr, n_ten, gsize),
        out_shape=jax.ShapeDtypeStruct((n_blk, span_rows, half), bf16),
        in_specs=[whole(pltpu.SMEM), whole(), whole()],
        out_specs=whole(),
        scratch_shapes=[pltpu.VMEM((groups // 2, round_up(2 * rows + span - 1, LANES)), f32)],
        compiler_params=limit(16),
        name="conv",
    )(lengths, taps, source)

    partial, *pages = lax.optimization_barrier((partial, *pages))
    parts = lax.all_to_all(
        partial,
        "blk",
        split_axis=0,
        concat_axis=0,
        axis_index_groups=[part_order(n_blk)],
        tiled=True,
    )

    stack = jax.ShapeDtypeStruct((n_chip, span_rows, width), bf16)
    head = jax.ShapeDtypeStruct((min(n_dev, -(-span // fr)), 2 * pairs, groups // 2), bf16)
    own_stack, own_head, bias = pl.pallas_call(
        functools.partial(gather_kernel, tap_order(n_blk, n_ten), fr, bias_width),
        out_shape=(stack, head, jax.ShapeDtypeStruct((1, width), f32)),
        in_specs=[whole(pl.ANY)] + [whole()] * (1 + n_chip),
        out_specs=(whole(),) * 3,
        compiler_params=limit(8),
        name="gather",
    )(partial, taps, *pages)
    peer_stack = lax.ppermute(own_stack, "blk", swap)
    peer_head = lax.ppermute(own_head, "blk", swap)

    extra, pool = pl.pallas_call(
        functools.partial(span_kernel, fr, gsize),
        out_shape=(
            jax.ShapeDtypeStruct((span_rows, width), f32),
            jax.ShapeDtypeStruct((MOST, PAGE, width), bf16),
        ),
        in_specs=[whole(pltpu.SMEM)] + [whole()] * 6,
        out_specs=(whole(), whole()),
        scratch_shapes=[
            pltpu.VMEM((groups, round_up(span + PAGE - 1, LANES)), f32),
            pltpu.VMEM((n_blk, span_rows, width), bf16),
        ],
        compiler_params=limit(8),
        name="span",
    )(page_owner.reshape(n_blk), own_stack, peer_stack, own_head, peer_head, inputs, bias)

    mixed = pl.pallas_call(
        finish_kernel,
        out_shape=jax.ShapeDtypeStruct((span_rows, width), bf16),
        in_specs=[whole()] * 3,
        out_specs=whole(),
        compiler_params=limit(8),
        name="finish",
    )(parts, span_gate[0], extra)
    return mixed[None], pool.reshape(1, MOST * PAGE, width)


def solution(mesh):
    return jax.shard_map(
        per_device,
        mesh=mesh,
        in_specs=(
            P("tenant", "blk", None),
            P("tenant", "blk", None),
            P("tenant", "blk", None),
            P("tenant", "blk", None),
            P(("blk", "tenant"), None),
            P(("blk", "tenant")),
            P("tenant"),
            P("tenant", None, None),
        ),
        out_specs=(P("tenant", "blk", None), P("tenant", "blk", None)),
        check_vma=False,
    )
```

```python
import functools

import jax
import jax.numpy as jnp
from jax import lax
from jax.experimental import pallas as pl
from jax.experimental.pallas import tpu as pltpu
from jax.sharding import PartitionSpec as P

PAGE = 8
MOST = 2
LANES = 128

bf16 = jnp.bfloat16
f32 = jnp.float32


def round_up(value, step):
    return -(-value // step) * step


def middle_out(count):
    low, high = list(range(count // 2))[::-1], list(range(count // 2, count))
    return [chip for pair in zip(low, high, strict=True) for chip in pair]


def part_order(n_blk):
    return [2 * chip + core for core in (1, 0) for chip in middle_out(n_blk // 2)[::-1]]


def tap_order(n_blk, n_ten):
    chips = middle_out(n_blk // 2)
    chips = chips[len(chips) // 2 :] + chips[: len(chips) // 2]
    return [
        (2 * chip + core) * n_ten + tenant
        for core in (1, 0)
        for chip in chips
        for tenant in range(n_ten)
    ]


def tap_place(number, n_blk, n_ten):
    order = tap_order(n_blk, n_ten)
    block, tenant = lax.div(number, n_ten), lax.rem(number, n_ten)
    core, chip = lax.rem(block, 2), lax.div(block, 2)
    place = jnp.int32(0)
    for each in range(n_blk // 2):
        place = jnp.where(chip == each, order.index((2 * each + 1) * n_ten), place)
    return place + (1 - core) * (len(order) // 2) + tenant


def pack_kernel(order, n_ten, taps_hbm, bias_hbm, send_ref, token_ref, *scratch):
    held, sems = scratch[:-1], scratch[-1]
    copies = [
        pltpu.make_async_copy(source, target, sems.at[i])
        for i, (source, target) in enumerate(zip((taps_hbm, bias_hbm), held, strict=True))
    ]
    for copy in copies:
        copy.start()
    token_ref[...] = jnp.zeros_like(token_ref)
    for copy in copies:
        copy.wait()
    taps_ref, bias_ref = held
    n_dev, pairs, _, lanes = send_ref.shape
    padded = 2 * pairs
    rows = taps_ref.shape[0]
    bias = bias_ref[...].astype(f32)
    if bias.shape[1] < lanes:
        bias = jnp.concatenate([bias, jnp.zeros((1, lanes - bias.shape[1]), f32)], axis=1)
    blocks = []
    for half in range(2):
        taps = taps_ref[:, half * lanes : (half + 1) * lanes].astype(f32)
        parts = [taps, bias]
        if padded > rows + 1:
            parts.append(jnp.zeros((padded - rows - 1, lanes), f32))
        blocks.append(jnp.concatenate(parts, axis=0).astype(bf16).reshape(pairs, 2, lanes))
    for place in range(n_dev):
        send_ref[place] = blocks[(order[place] // n_ten) % 2]


def input_kernel(_, key_ref, value_ref, input_ref):
    input_ref[...] = (key_ref[...].astype(f32) * value_ref[...].astype(f32)).astype(bf16)


def source_kernel(len_ref, own_ref, *refs):
    peer_refs, out_ref = refs[:-1], refs[-1]
    blk = lax.axis_index("blk")
    core = lax.rem(blk, 2)
    rows, width = own_ref.shape
    start = (blk - core) * rows
    length = len_ref[0]

    def masked(value, first):
        index = first + lax.broadcasted_iota(jnp.int32, value.shape, 0)
        return jnp.where(index < length, value.astype(f32), 0.0).astype(bf16)

    own_at = pl.multiple_of(core * rows, rows)
    out_ref[pl.ds(own_at, rows), :] = masked(own_ref[...], start + core * rows)
    piece = rows // len(peer_refs)
    for i, peer_ref in enumerate(peer_refs):
        peer_at = pl.multiple_of((1 - core) * rows + i * piece, piece)
        out_ref[pl.ds(peer_at, piece), :] = masked(peer_ref[...], start + peer_at)


def reversed_taps(window, first, fr, top_lag, lanes):
    blocks, padded, groups = window.shape
    shape = (blocks * padded, lanes)
    index = lax.broadcasted_iota(jnp.int32, shape, 0)
    lane = lax.broadcasted_iota(jnp.int32, shape, 1)
    block = lax.div(index * ((1 << 16) // padded + 1), 1 << 16)
    row = index - block * padded
    lag = (first + block) * fr + row
    pick = jnp.where((row < fr) & (lag + lane == top_lag), 1.0, 0.0).astype(bf16)
    return lax.dot_general(
        window.reshape(blocks * padded, groups),
        pick,
        (((0,), (0,)), ((), ())),
        preferred_element_type=f32,
    )


def toeplitz_product(taps_ref, first_group, gsize, outputs, depth, source):
    per = LANES // gsize
    lanes = taps_ref.shape[1]
    tiles = []
    for g in range(per):
        line = jnp.broadcast_to(taps_ref[pl.ds(first_group + g, 1), :], (outputs, lanes))
        line = pltpu.roll(line, lanes - (outputs - 1), 1, stride=1, stride_axis=0)
        tiles.append(line[:, :depth])
    matrix = jnp.concatenate(tiles, axis=0).astype(bf16)
    product = jnp.dot(matrix, source, preferred_element_type=f32)
    group = lax.broadcasted_iota(jnp.int32, (outputs, LANES), 1) // gsize
    total = product[:outputs]
    for g in range(1, per):
        total = jnp.where(group == g, product[g * outputs : (g + 1) * outputs], total)
    return total


def conv_kernel(fr, n_ten, gsize, len_ref, taps_ref, source_ref, out_ref, line_ref):
    n_dev, pairs, _, groups = taps_ref.shape
    n_blk, page, _ = out_ref.shape
    span = n_blk * page
    rows = source_ref.shape[0]
    base = len_ref[0] - lax.div(lax.axis_index("blk"), 2) * rows
    blocks = min(n_dev, -(-(fr - 1 + rows + span - 1) // fr))
    low = jnp.maximum(base - rows + 1, 0)
    first = jnp.clip(lax.div(low, fr), 0, n_dev - blocks)
    window = [
        taps_ref[tap_place(first + i, n_blk, n_ten)].reshape(2 * pairs, groups)
        for i in range(blocks)
    ]
    line_ref[...] = reversed_taps(
        jnp.stack(window), first, fr, base + span - 1, line_ref.shape[1]
    )
    per = LANES // gsize
    for index in range(groups // per):
        columns = slice(index * LANES, (index + 1) * LANES)
        total = toeplitz_product(
            line_ref, index * per, gsize, span, rows, source_ref[:, columns]
        )
        for place, block in enumerate(part_order(n_blk)):
            out_ref[place, :, columns] = total[block * page : (block + 1) * page].astype(bf16)


def gather_kernel(order, fr, bias_width, _, taps_ref, *refs):
    pages, (stack_ref, head_ref, bias_ref) = refs[:-3], refs[-3:]
    chip = lax.div(lax.axis_index("blk"), 2)
    for step, page in enumerate(pages):
        stack_ref[lax.bitwise_xor(chip, step)] = page[...]
    for index in range(head_ref.shape[0]):
        head_ref[index] = taps_ref[order.index(index)].reshape(head_ref.shape[1:])
    each = LANES // bias_width
    for index in range(taps_ref.shape[0] // each):
        row = [
            taps_ref[order.index(index * each + i), fr // 2, fr % 2 : fr % 2 + 1, :bias_width].astype(f32)
            for i in range(each)
        ]
        row = row[0] if each == 1 else jnp.concatenate(row, axis=1)
        bias_ref[:, index * LANES : (index + 1) * LANES] = row


def span_kernel(
    fr,
    gsize,
    owner_ref,
    own_stack_ref,
    peer_stack_ref,
    own_head_ref,
    peer_head_ref,
    input_ref,
    bias_ref,
    extra_ref,
    pool_ref,
    line_ref,
    source_ref,
):
    blk = lax.axis_index("blk")
    core = lax.rem(blk, 2)
    n_chip, page, width = own_stack_ref.shape
    n_blk = 2 * n_chip
    pool_ref[...] = jnp.zeros_like(pool_ref)
    for chip in range(n_chip):
        for stack, side in ((own_stack_ref, core), (peer_stack_ref, 1 - core)):
            number = 2 * chip + side
            value = stack[chip]
            source_ref[number] = value
            owner = owner_ref[number]
            rank = jnp.int32(0)
            for other in range(n_blk):
                earlier = (owner_ref[other] == owner) & (other < number)
                rank = rank + earlier.astype(jnp.int32)

            @pl.when(owner == blk)
            def _(value=value, rank=rank):
                pool_ref[rank] = value

    groups = own_head_ref.shape[2]
    lanes = line_ref.shape[1]
    top_lag = blk * page + page - 1
    for head, side in ((own_head_ref, core), (peer_head_ref, 1 - core)):
        at = pl.multiple_of(side * groups, groups)
        line_ref[pl.ds(at, groups), :] = reversed_taps(head[...], 0, fr, top_lag, lanes)
    per = LANES // gsize
    for index in range(width // LANES):
        columns = slice(index * LANES, (index + 1) * LANES)
        source = source_ref[:, :, columns].reshape(n_blk * page, LANES)
        total = toeplitz_product(line_ref, index * per, gsize, page, n_blk * page, source)
        skip = bias_ref[:, columns] * input_ref[:, columns].astype(f32)
        extra_ref[:, columns] = total + skip


def finish_kernel(parts_ref, gate_ref, extra_ref, mixed_ref):
    n_blk, _, half = parts_ref.shape
    for core in range(2):
        columns = slice(core * half, (core + 1) * half)
        total = extra_ref[:, columns]
        for place, block in enumerate(part_order(n_blk)):
            if block % 2 == core:
                total = total + parts_ref[place].astype(f32)
        gate = gate_ref[:, columns].astype(f32)
        mixed_ref[:, columns] = (gate * total).astype(bf16)


def whole(memory=pltpu.VMEM):
    return pl.BlockSpec(memory_space=memory)


def limit(mebibytes):
    return pltpu.CompilerParams(vmem_limit_bytes=mebibytes << 20)


def per_device(
    history_u, span_gate, span_key, span_value, filter_taps, skip_bias, lengths, page_owner
):
    n_blk, n_ten = lax.axis_size("blk"), lax.axis_size("tenant")
    n_dev, n_chip = n_blk * n_ten, n_blk // 2
    history = history_u[0]
    rows, width = history.shape
    half = width // 2
    span_rows = span_key.shape[1]
    span = span_rows * n_blk
    fr, groups = filter_taps.shape
    gsize = width // groups
    pairs = round_up(fr + 1, 2) // 2
    bias_width = skip_bias.shape[0]
    swap = [(i, i ^ 1) for i in range(n_blk)]

    send, token = pl.pallas_call(
        functools.partial(pack_kernel, tap_order(n_blk, n_ten), n_ten),
        out_shape=(
            jax.ShapeDtypeStruct((n_dev, pairs, 2, groups // 2), bf16),
            jax.ShapeDtypeStruct((8, LANES), f32),
        ),
        in_specs=[whole(pltpu.HBM)] * 2,
        out_specs=(whole(), whole()),
        scratch_shapes=[
            pltpu.VMEM((fr, groups), bf16),
            pltpu.VMEM((1, bias_width), bf16),
            pltpu.SemaphoreType.DMA((2,)),
        ],
        compiler_params=limit(58),
        name="pack",
    )(filter_taps, skip_bias.reshape(1, bias_width))
    taps = lax.all_to_all(
        send,
        ("blk", "tenant"),
        split_axis=0,
        concat_axis=0,
        axis_index_groups=[tap_order(n_blk, n_ten)],
        tiled=True,
    )
    pieces = 4
    piece = rows // pieces
    peer_history = [
        lax.ppermute(history[i * piece : (i + 1) * piece], "blk", swap) for i in range(pieces)
    ]

    def half_block(count):
        return pl.BlockSpec((count, half), lambda i, n: (0, lax.rem(lax.axis_index("blk"), 2)))

    source = pl.pallas_call(
        source_kernel,
        grid_spec=pltpu.PrefetchScalarGridSpec(
            num_scalar_prefetch=1,
            grid=(1,),
            in_specs=[half_block(rows)] + [half_block(piece)] * pieces,
            out_specs=pl.BlockSpec((2 * rows, half), lambda i, n: (0, 0)),
        ),
        out_shape=jax.ShapeDtypeStruct((2 * rows, half), bf16),
        compiler_params=limit(8),
        name="source",
    )(lengths, history, *peer_history)

    inputs = pl.pallas_call(
        input_kernel,
        out_shape=jax.ShapeDtypeStruct((span_rows, width), bf16),
        in_specs=[whole(pl.ANY)] + [whole()] * 2,
        out_specs=whole(),
        compiler_params=limit(8),
        cost_estimate=pl.CostEstimate(flops=32768, bytes_accessed=3 * span_rows * width * 2, transcendentals=0),
        name="inputs",
    )(source, span_key[0], span_value[0])

    pages = [inputs]
    for step in range(1, n_chip):
        turn = [(i, i ^ (2 * step)) for i in range(n_blk)]
        pages.append(lax.ppermute(inputs, "blk", turn))
    partial = pl.pallas_call(
        functools.partial(conv_kernel, fr, n_ten, gsize),
        out_shape=jax.ShapeDtypeStruct((n_blk, span_rows, half), bf16),
        in_specs=[whole(pltpu.SMEM), whole(), whole()],
        out_specs=whole(),
        scratch_shapes=[pltpu.VMEM((groups // 2, round_up(2 * rows + span - 1, LANES)), f32)],
        compiler_params=limit(16),
        name="conv",
    )(lengths, taps, source)

    partial, *pages = lax.optimization_barrier((partial, *pages))
    parts = lax.all_to_all(
        partial,
        "blk",
        split_axis=0,
        concat_axis=0,
        axis_index_groups=[part_order(n_blk)],
        tiled=True,
    )

    stack = jax.ShapeDtypeStruct((n_chip, span_rows, width), bf16)
    head = jax.ShapeDtypeStruct((min(n_dev, -(-span // fr)), 2 * pairs, groups // 2), bf16)
    own_stack, own_head, bias = pl.pallas_call(
        functools.partial(gather_kernel, tap_order(n_blk, n_ten), fr, bias_width),
        out_shape=(stack, head, jax.ShapeDtypeStruct((1, width), f32)),
        in_specs=[whole(pl.ANY)] + [whole()] * (1 + n_chip),
        out_specs=(whole(),) * 3,
        compiler_params=limit(8),
        name="gather",
    )(partial, taps, *pages)
    peer_stack = lax.ppermute(own_stack, "blk", swap)
    peer_head = lax.ppermute(own_head, "blk", swap)

    extra, pool = pl.pallas_call(
        functools.partial(span_kernel, fr, gsize),
        out_shape=(
            jax.ShapeDtypeStruct((span_rows, width), f32),
            jax.ShapeDtypeStruct((MOST, PAGE, width), bf16),
        ),
        in_specs=[whole(pltpu.SMEM)] + [whole()] * 6,
        out_specs=(whole(), whole()),
        scratch_shapes=[
            pltpu.VMEM((groups, round_up(span + PAGE - 1, LANES)), f32),
            pltpu.VMEM((n_blk, span_rows, width), bf16),
        ],
        compiler_params=limit(8),
        name="span",
    )(page_owner.reshape(n_blk), own_stack, peer_stack, own_head, peer_head, inputs, bias)

    mixed = pl.pallas_call(
        finish_kernel,
        out_shape=jax.ShapeDtypeStruct((span_rows, width), bf16),
        in_specs=[whole()] * 3,
        out_specs=whole(),
        compiler_params=limit(8),
        name="finish",
    )(parts, span_gate[0], extra)
    return mixed[None], pool.reshape(1, MOST * PAGE, width)


def solution(mesh):
    return jax.shard_map(
        per_device,
        mesh=mesh,
        in_specs=(
            P("tenant", "blk", None),
            P("tenant", "blk", None),
            P("tenant", "blk", None),
            P("tenant", "blk", None),
            P(("blk", "tenant"), None),
            P(("blk", "tenant")),
            P("tenant"),
            P("tenant", None, None),
        ),
        out_specs=(P("tenant", "blk", None), P("tenant", "blk", None)),
        check_vma=False,
    )
```

```python
import functools

import jax
import jax.numpy as jnp
from jax import lax
from jax.experimental import pallas as pl
from jax.experimental.pallas import tpu as pltpu
from jax.sharding import PartitionSpec as P

PAGE = 8
MOST = 2
LANES = 128
OUT_COPIES = 4

bf16 = jnp.bfloat16
f32 = jnp.float32


def round_up(value, step):
    return -(-value // step) * step


def middle_out(count):
    low, high = list(range(count // 2))[::-1], list(range(count // 2, count))
    return [chip for pair in zip(low, high, strict=True) for chip in pair]


def part_order(n_blk):
    return [2 * chip + core for core in (1, 0) for chip in middle_out(n_blk // 2)[::-1]]


def tap_order(n_blk, n_ten):
    chips = middle_out(n_blk // 2)
    chips = chips[len(chips) // 2 :] + chips[: len(chips) // 2]
    return [
        (2 * chip + core) * n_ten + tenant
        for core in (1, 0)
        for chip in chips
        for tenant in range(n_ten)
    ]


def tap_place(number, n_blk, n_ten):
    order = tap_order(n_blk, n_ten)
    block, tenant = lax.div(number, n_ten), lax.rem(number, n_ten)
    core, chip = lax.rem(block, 2), lax.div(block, 2)
    place = jnp.int32(0)
    for each in range(n_blk // 2):
        place = jnp.where(chip == each, order.index((2 * each + 1) * n_ten), place)
    return place + (1 - core) * (len(order) // 2) + tenant


def pack_kernel(order, n_ten, taps_hbm, bias_hbm, send_ref, token_ref, *scratch):
    held, sems = scratch[:-1], scratch[-1]
    copies = [
        pltpu.make_async_copy(source, target, sems.at[i])
        for i, (source, target) in enumerate(zip((taps_hbm, bias_hbm), held, strict=True))
    ]
    for copy in copies:
        copy.start()
    token_ref[...] = jnp.zeros_like(token_ref)
    for copy in copies:
        copy.wait()
    taps_ref, bias_ref = held
    n_dev, pairs, _, lanes = send_ref.shape
    padded = 2 * pairs
    rows = taps_ref.shape[0]
    bias = bias_ref[...].astype(f32)
    if bias.shape[1] < lanes:
        bias = jnp.concatenate([bias, jnp.zeros((1, lanes - bias.shape[1]), f32)], axis=1)
    blocks = []
    for half in range(2):
        taps = taps_ref[:, half * lanes : (half + 1) * lanes].astype(f32)
        parts = [taps, bias]
        if padded > rows + 1:
            parts.append(jnp.zeros((padded - rows - 1, lanes), f32))
        blocks.append(jnp.concatenate(parts, axis=0).astype(bf16).reshape(pairs, 2, lanes))
    for place in range(n_dev):
        send_ref[place] = blocks[(order[place] // n_ten) % 2]


def input_kernel(_, key_ref, value_ref, input_ref):
    input_ref[...] = (key_ref[...].astype(f32) * value_ref[...].astype(f32)).astype(bf16)


def source_kernel(len_ref, own_ref, *refs):
    peer_refs, out_ref = refs[:-1], refs[-1]
    blk = lax.axis_index("blk")
    core = lax.rem(blk, 2)
    rows, width = own_ref.shape
    start = (blk - core) * rows
    length = len_ref[0]

    def masked(value, first):
        index = first + lax.broadcasted_iota(jnp.int32, value.shape, 0)
        return jnp.where(index < length, value.astype(f32), 0.0).astype(bf16)

    own_at = pl.multiple_of(core * rows, rows)
    out_ref[pl.ds(own_at, rows), :] = masked(own_ref[...], start + core * rows)
    piece = rows // len(peer_refs)
    for i, peer_ref in enumerate(peer_refs):
        peer_at = pl.multiple_of((1 - core) * rows + i * piece, piece)
        out_ref[pl.ds(peer_at, piece), :] = masked(peer_ref[...], start + peer_at)


def reversed_taps(window, first, fr, top_lag, lanes):
    blocks, padded, groups = window.shape
    shape = (blocks * padded, lanes)
    index = lax.broadcasted_iota(jnp.int32, shape, 0)
    lane = lax.broadcasted_iota(jnp.int32, shape, 1)
    block = lax.div(index * ((1 << 16) // padded + 1), 1 << 16)
    row = index - block * padded
    lag = (first + block) * fr + row
    pick = jnp.where((row < fr) & (lag + lane == top_lag), 1.0, 0.0).astype(bf16)
    return lax.dot_general(
        window.reshape(blocks * padded, groups),
        pick,
        (((0,), (0,)), ((), ())),
        preferred_element_type=f32,
    )


def toeplitz_product(taps_ref, first_group, gsize, outputs, depth, source):
    per = LANES // gsize
    lanes = taps_ref.shape[1]
    tiles = []
    for g in range(per):
        line = jnp.broadcast_to(taps_ref[pl.ds(first_group + g, 1), :], (outputs, lanes))
        line = pltpu.roll(line, lanes - (outputs - 1), 1, stride=1, stride_axis=0)
        tiles.append(line[:, :depth])
    matrix = jnp.concatenate(tiles, axis=0).astype(bf16)
    product = jnp.dot(matrix, source, preferred_element_type=f32)
    group = lax.broadcasted_iota(jnp.int32, (outputs, LANES), 1) // gsize
    total = product[:outputs]
    for g in range(1, per):
        total = jnp.where(group == g, product[g * outputs : (g + 1) * outputs], total)
    return total


def conv_kernel(fr, n_ten, gsize, len_ref, taps_ref, source_ref, out_hbm, line_ref, out_ref, sems):
    n_dev, pairs, _, groups = taps_ref.shape
    n_blk, page, _ = out_ref.shape
    span = n_blk * page
    rows = source_ref.shape[0]
    base = len_ref[0] - lax.div(lax.axis_index("blk"), 2) * rows
    blocks = min(n_dev, -(-(fr - 1 + rows + span - 1) // fr))
    low = jnp.maximum(base - rows + 1, 0)
    first = jnp.clip(lax.div(low, fr), 0, n_dev - blocks)
    window = [
        taps_ref[tap_place(first + i, n_blk, n_ten)].reshape(2 * pairs, groups)
        for i in range(blocks)
    ]
    line_ref[...] = reversed_taps(
        jnp.stack(window), first, fr, base + span - 1, line_ref.shape[1]
    )
    per = LANES // gsize
    every, copies = groups // per // OUT_COPIES, []
    for index in range(groups // per):
        columns = slice(index * LANES, (index + 1) * LANES)
        total = toeplitz_product(
            line_ref, index * per, gsize, span, rows, source_ref[:, columns]
        )
        for place, block in enumerate(part_order(n_blk)):
            out_ref[place, :, columns] = total[block * page : (block + 1) * page].astype(bf16)
        if (index + 1) % every == 0:
            done = slice((index + 1 - every) * LANES, (index + 1) * LANES)
            copies.append(
                pltpu.make_async_copy(
                    out_ref.at[:, :, done], out_hbm.at[:, :, done], sems.at[len(copies)]
                )
            )
            copies[-1].start()
    for copy in copies:
        copy.wait()


def gather_kernel(order, fr, bias_width, _, taps_ref, *refs):
    pages, (stack_ref, head_ref, bias_ref) = refs[:-3], refs[-3:]
    chip = lax.div(lax.axis_index("blk"), 2)
    for step, page in enumerate(pages):
        stack_ref[lax.bitwise_xor(chip, step)] = page[...]
    for index in range(head_ref.shape[0]):
        head_ref[index] = taps_ref[order.index(index)].reshape(head_ref.shape[1:])
    each = LANES // bias_width
    for index in range(taps_ref.shape[0] // each):
        row = [
            taps_ref[order.index(index * each + i), fr // 2, fr % 2 : fr % 2 + 1, :bias_width].astype(f32)
            for i in range(each)
        ]
        row = row[0] if each == 1 else jnp.concatenate(row, axis=1)
        bias_ref[:, index * LANES : (index + 1) * LANES] = row


def span_kernel(
    fr,
    gsize,
    owner_ref,
    own_stack_ref,
    peer_stack_ref,
    own_head_ref,
    peer_head_ref,
    input_ref,
    bias_ref,
    extra_ref,
    pool_ref,
    line_ref,
    source_ref,
):
    blk = lax.axis_index("blk")
    core = lax.rem(blk, 2)
    n_chip, page, width = own_stack_ref.shape
    n_blk = 2 * n_chip
    pool_ref[...] = jnp.zeros_like(pool_ref)
    for chip in range(n_chip):
        for stack, side in ((own_stack_ref, core), (peer_stack_ref, 1 - core)):
            number = 2 * chip + side
            value = stack[chip]
            source_ref[number] = value
            owner = owner_ref[number]
            rank = jnp.int32(0)
            for other in range(n_blk):
                earlier = (owner_ref[other] == owner) & (other < number)
                rank = rank + earlier.astype(jnp.int32)

            @pl.when(owner == blk)
            def _(value=value, rank=rank):
                pool_ref[rank] = value

    groups = own_head_ref.shape[2]
    lanes = line_ref.shape[1]
    top_lag = blk * page + page - 1
    for head, side in ((own_head_ref, core), (peer_head_ref, 1 - core)):
        at = pl.multiple_of(side * groups, groups)
        line_ref[pl.ds(at, groups), :] = reversed_taps(head[...], 0, fr, top_lag, lanes)
    per = LANES // gsize
    for index in range(width // LANES):
        columns = slice(index * LANES, (index + 1) * LANES)
        source = source_ref[:, :, columns].reshape(n_blk * page, LANES)
        total = toeplitz_product(line_ref, index * per, gsize, page, n_blk * page, source)
        skip = bias_ref[:, columns] * input_ref[:, columns].astype(f32)
        extra_ref[:, columns] = total + skip


def finish_kernel(parts_ref, gate_ref, extra_ref, mixed_ref):
    n_blk, _, half = parts_ref.shape
    for core in range(2):
        columns = slice(core * half, (core + 1) * half)
        total = extra_ref[:, columns]
        for place, block in enumerate(part_order(n_blk)):
            if block % 2 == core:
                total = total + parts_ref[place].astype(f32)
        gate = gate_ref[:, columns].astype(f32)
        mixed_ref[:, columns] = (gate * total).astype(bf16)


def whole(memory=pltpu.VMEM):
    return pl.BlockSpec(memory_space=memory)


def limit(mebibytes):
    return pltpu.CompilerParams(vmem_limit_bytes=mebibytes << 20)


def per_device(
    history_u, span_gate, span_key, span_value, filter_taps, skip_bias, lengths, page_owner
):
    n_blk, n_ten = lax.axis_size("blk"), lax.axis_size("tenant")
    n_dev, n_chip = n_blk * n_ten, n_blk // 2
    history = history_u[0]
    rows, width = history.shape
    half = width // 2
    span_rows = span_key.shape[1]
    span = span_rows * n_blk
    fr, groups = filter_taps.shape
    gsize = width // groups
    pairs = round_up(fr + 1, 2) // 2
    bias_width = skip_bias.shape[0]
    swap = [(i, i ^ 1) for i in range(n_blk)]

    send, token = pl.pallas_call(
        functools.partial(pack_kernel, tap_order(n_blk, n_ten), n_ten),
        out_shape=(
            jax.ShapeDtypeStruct((n_dev, pairs, 2, groups // 2), bf16),
            jax.ShapeDtypeStruct((8, LANES), f32),
        ),
        in_specs=[whole(pltpu.HBM)] * 2,
        out_specs=(whole(), whole()),
        scratch_shapes=[
            pltpu.VMEM((fr, groups), bf16),
            pltpu.VMEM((1, bias_width), bf16),
            pltpu.SemaphoreType.DMA((2,)),
        ],
        compiler_params=limit(58),
        name="pack",
    )(filter_taps, skip_bias.reshape(1, bias_width))
    taps = lax.all_to_all(
        send,
        ("blk", "tenant"),
        split_axis=0,
        concat_axis=0,
        axis_index_groups=[tap_order(n_blk, n_ten)],
        tiled=True,
    )
    pieces = 4
    piece = rows // pieces
    peer_history = [
        lax.ppermute(history[i * piece : (i + 1) * piece], "blk", swap) for i in range(pieces)
    ]

    def half_block(count):
        return pl.BlockSpec((count, half), lambda i, n: (0, lax.rem(lax.axis_index("blk"), 2)))

    source = pl.pallas_call(
        source_kernel,
        grid_spec=pltpu.PrefetchScalarGridSpec(
            num_scalar_prefetch=1,
            grid=(1,),
            in_specs=[half_block(rows)] + [half_block(piece)] * pieces,
            out_specs=pl.BlockSpec((2 * rows, half), lambda i, n: (0, 0)),
        ),
        out_shape=jax.ShapeDtypeStruct((2 * rows, half), bf16),
        compiler_params=limit(8),
        name="source",
    )(lengths, history, *peer_history)

    inputs = pl.pallas_call(
        input_kernel,
        out_shape=jax.ShapeDtypeStruct((span_rows, width), bf16),
        in_specs=[whole(pl.ANY)] + [whole()] * 2,
        out_specs=whole(),
        compiler_params=limit(8),
        cost_estimate=pl.CostEstimate(flops=32768, bytes_accessed=3 * span_rows * width * 2, transcendentals=0),
        name="inputs",
    )(source, span_key[0], span_value[0])

    pages = [inputs]
    for step in range(1, n_chip):
        turn = [(i, i ^ (2 * step)) for i in range(n_blk)]
        pages.append(lax.ppermute(inputs, "blk", turn))
    partial = pl.pallas_call(
        functools.partial(conv_kernel, fr, n_ten, gsize),
        out_shape=jax.ShapeDtypeStruct((n_blk, span_rows, half), bf16),
        in_specs=[whole(pltpu.SMEM), whole(), whole()],
        out_specs=whole(pltpu.HBM),
        scratch_shapes=[
            pltpu.VMEM((groups // 2, round_up(2 * rows + span - 1, LANES)), f32),
            pltpu.VMEM((n_blk, span_rows, half), bf16),
            pltpu.SemaphoreType.DMA((OUT_COPIES,)),
        ],
        compiler_params=limit(16),
        name="conv",
    )(lengths, taps, source)

    partial, *pages = lax.optimization_barrier((partial, *pages))
    parts = lax.all_to_all(
        partial,
        "blk",
        split_axis=0,
        concat_axis=0,
        axis_index_groups=[part_order(n_blk)],
        tiled=True,
    )

    stack = jax.ShapeDtypeStruct((n_chip, span_rows, width), bf16)
    head = jax.ShapeDtypeStruct((min(n_dev, -(-span // fr)), 2 * pairs, groups // 2), bf16)
    own_stack, own_head, bias = pl.pallas_call(
        functools.partial(gather_kernel, tap_order(n_blk, n_ten), fr, bias_width),
        out_shape=(stack, head, jax.ShapeDtypeStruct((1, width), f32)),
        in_specs=[whole(pl.ANY)] + [whole()] * (1 + n_chip),
        out_specs=(whole(),) * 3,
        compiler_params=limit(8),
        name="gather",
    )(partial, taps, *pages)
    peer_stack = lax.ppermute(own_stack, "blk", swap)
    peer_head = lax.ppermute(own_head, "blk", swap)

    extra, pool = pl.pallas_call(
        functools.partial(span_kernel, fr, gsize),
        out_shape=(
            jax.ShapeDtypeStruct((span_rows, width), f32),
            jax.ShapeDtypeStruct((MOST, PAGE, width), bf16),
        ),
        in_specs=[whole(pltpu.SMEM)] + [whole()] * 6,
        out_specs=(whole(), whole()),
        scratch_shapes=[
            pltpu.VMEM((groups, round_up(span + PAGE - 1, LANES)), f32),
            pltpu.VMEM((n_blk, span_rows, width), bf16),
        ],
        compiler_params=limit(8),
        name="span",
    )(page_owner.reshape(n_blk), own_stack, peer_stack, own_head, peer_head, inputs, bias)

    mixed = pl.pallas_call(
        finish_kernel,
        out_shape=jax.ShapeDtypeStruct((span_rows, width), bf16),
        in_specs=[whole()] * 3,
        out_specs=whole(),
        compiler_params=limit(8),
        name="finish",
    )(parts, span_gate[0], extra)
    return mixed[None], pool.reshape(1, MOST * PAGE, width)


def solution(mesh):
    return jax.shard_map(
        per_device,
        mesh=mesh,
        in_specs=(
            P("tenant", "blk", None),
            P("tenant", "blk", None),
            P("tenant", "blk", None),
            P("tenant", "blk", None),
            P(("blk", "tenant"), None),
            P(("blk", "tenant")),
            P("tenant"),
            P("tenant", None, None),
        ),
        out_specs=(P("tenant", "blk", None), P("tenant", "blk", None)),
        check_vma=False,
    )
```

```python
import functools

import jax
import jax.numpy as jnp
from jax import lax
from jax.experimental import pallas as pl
from jax.experimental.pallas import tpu as pltpu
from jax.sharding import PartitionSpec as P

PAGE = 8
MOST = 2
LANES = 128
OUT_COPIES = 4

bf16 = jnp.bfloat16
f32 = jnp.float32


def round_up(value, step):
    return -(-value // step) * step


def middle_out(count):
    low, high = list(range(count // 2))[::-1], list(range(count // 2, count))
    return [chip for pair in zip(low, high, strict=True) for chip in pair]


def part_order(n_blk):
    return [2 * chip + core for core in (1, 0) for chip in middle_out(n_blk // 2)[::-1]]


def tap_order(n_blk, n_ten):
    chips = middle_out(n_blk // 2)
    chips = chips[len(chips) // 2 :] + chips[: len(chips) // 2]
    return [
        (2 * chip + core) * n_ten + tenant
        for core in (1, 0)
        for chip in chips
        for tenant in range(n_ten)
    ]


def tap_place(number, n_blk, n_ten):
    order = tap_order(n_blk, n_ten)
    block, tenant = lax.div(number, n_ten), lax.rem(number, n_ten)
    core, chip = lax.rem(block, 2), lax.div(block, 2)
    place = jnp.int32(0)
    for each in range(n_blk // 2):
        place = jnp.where(chip == each, order.index((2 * each + 1) * n_ten), place)
    return place + (1 - core) * (len(order) // 2) + tenant


def pack_kernel(order, n_ten, taps_hbm, bias_hbm, send_ref, token_ref, *scratch):
    held, sems = scratch[:-1], scratch[-1]
    copies = [
        pltpu.make_async_copy(source, target, sems.at[i])
        for i, (source, target) in enumerate(zip((taps_hbm, bias_hbm), held, strict=True))
    ]
    for copy in copies:
        copy.start()
    token_ref[...] = jnp.zeros_like(token_ref)
    for copy in copies:
        copy.wait()
    taps_ref, bias_ref = held
    n_dev, pairs, _, lanes = send_ref.shape
    padded = 2 * pairs
    rows = taps_ref.shape[0]
    bias = bias_ref[...].astype(f32)
    if bias.shape[1] < lanes:
        bias = jnp.concatenate([bias, jnp.zeros((1, lanes - bias.shape[1]), f32)], axis=1)
    blocks = []
    for half in range(2):
        taps = taps_ref[:, half * lanes : (half + 1) * lanes].astype(f32)
        parts = [taps, bias]
        if padded > rows + 1:
            parts.append(jnp.zeros((padded - rows - 1, lanes), f32))
        blocks.append(jnp.concatenate(parts, axis=0).astype(bf16).reshape(pairs, 2, lanes))
    for place in range(n_dev):
        send_ref[place] = blocks[(order[place] // n_ten) % 2]


def input_kernel(_, key_ref, value_ref, input_ref):
    input_ref[...] = (key_ref[...].astype(f32) * value_ref[...].astype(f32)).astype(bf16)


def source_kernel(len_ref, own_ref, *refs):
    peer_refs, out_ref = refs[:-1], refs[-1]
    blk = lax.axis_index("blk")
    core = lax.rem(blk, 2)
    rows, width = own_ref.shape
    start = (blk - core) * rows
    length = len_ref[0]

    def masked(value, first):
        index = first + lax.broadcasted_iota(jnp.int32, value.shape, 0)
        return jnp.where(index < length, value.astype(f32), 0.0).astype(bf16)

    own_at = pl.multiple_of(core * rows, rows)
    out_ref[pl.ds(own_at, rows), :] = masked(own_ref[...], start + core * rows)
    piece = rows // len(peer_refs)
    for i, peer_ref in enumerate(peer_refs):
        peer_at = pl.multiple_of((1 - core) * rows + i * piece, piece)
        out_ref[pl.ds(peer_at, piece), :] = masked(peer_ref[...], start + peer_at)


def reversed_taps(window, first, fr, top_lag, lanes):
    blocks, padded, groups = window.shape
    shape = (blocks * padded, lanes)
    index = lax.broadcasted_iota(jnp.int32, shape, 0)
    lane = lax.broadcasted_iota(jnp.int32, shape, 1)
    block = lax.div(index * ((1 << 16) // padded + 1), 1 << 16)
    row = index - block * padded
    lag = (first + block) * fr + row
    pick = jnp.where((row < fr) & (lag + lane == top_lag), 1.0, 0.0).astype(bf16)
    return lax.dot_general(
        window.reshape(blocks * padded, groups),
        pick,
        (((0,), (0,)), ((), ())),
        preferred_element_type=f32,
    )


def toeplitz_product(taps_ref, first_group, gsize, outputs, depth, source):
    per = LANES // gsize
    lanes = taps_ref.shape[1]
    shift = outputs - 1 - lax.broadcasted_iota(jnp.int32, (outputs, LANES), 0)
    inside = lax.broadcasted_iota(jnp.int32, (outputs, LANES), 1) + shift < LANES
    tiles = []
    for g in range(per):
        line = jnp.broadcast_to(taps_ref[pl.ds(first_group + g, 1), :], (outputs, lanes))
        if depth % LANES or lanes != depth + LANES or outputs > LANES:
            line = pltpu.roll(line, lanes - (outputs - 1), 1, stride=1, stride_axis=0)
            tiles.append(line[:, :depth])
            continue
        turned = [
            pltpu.roll(
                line[:, at : at + LANES], LANES - (outputs - 1), 1, stride=1, stride_axis=0
            )
            for at in range(0, lanes, LANES)
        ]
        pieces = [jnp.where(inside, a, b) for a, b in zip(turned[:-1], turned[1:], strict=True)]
        tiles.append(jnp.concatenate(pieces, axis=1))
    matrix = jnp.concatenate(tiles, axis=0).astype(bf16)
    product = jnp.dot(matrix, source, preferred_element_type=f32)
    group = lax.broadcasted_iota(jnp.int32, (outputs, LANES), 1) // gsize
    total = product[:outputs]
    for g in range(1, per):
        total = jnp.where(group == g, product[g * outputs : (g + 1) * outputs], total)
    return total


def conv_kernel(fr, n_ten, gsize, len_ref, taps_ref, source_ref, out_hbm, line_ref, out_ref, sems):
    n_dev, pairs, _, groups = taps_ref.shape
    n_blk, page, _ = out_ref.shape
    span = n_blk * page
    rows = source_ref.shape[0]
    base = len_ref[0] - lax.div(lax.axis_index("blk"), 2) * rows
    blocks = min(n_dev, -(-(fr - 1 + rows + span - 1) // fr))
    low = jnp.maximum(base - rows + 1, 0)
    first = jnp.clip(lax.div(low, fr), 0, n_dev - blocks)
    window = [
        taps_ref[tap_place(first + i, n_blk, n_ten)].reshape(2 * pairs, groups)
        for i in range(blocks)
    ]
    line_ref[...] = reversed_taps(
        jnp.stack(window), first, fr, base + span - 1, line_ref.shape[1]
    )
    per = LANES // gsize
    every, copies = groups // per // OUT_COPIES, []
    for index in range(groups // per):
        columns = slice(index * LANES, (index + 1) * LANES)
        total = toeplitz_product(
            line_ref, index * per, gsize, span, rows, source_ref[:, columns]
        )
        for place, block in enumerate(part_order(n_blk)):
            out_ref[place, :, columns] = total[block * page : (block + 1) * page].astype(bf16)
        if (index + 1) % every == 0:
            done = slice((index + 1 - every) * LANES, (index + 1) * LANES)
            copies.append(
                pltpu.make_async_copy(
                    out_ref.at[:, :, done], out_hbm.at[:, :, done], sems.at[len(copies)]
                )
            )
            copies[-1].start()
    for copy in copies:
        copy.wait()


def gather_kernel(order, fr, bias_width, _, taps_ref, *refs):
    pages, (stack_ref, head_ref, bias_ref) = refs[:-3], refs[-3:]
    chip = lax.div(lax.axis_index("blk"), 2)
    for step, page in enumerate(pages):
        stack_ref[lax.bitwise_xor(chip, step)] = page[...]
    for index in range(head_ref.shape[0]):
        head_ref[index] = taps_ref[order.index(index)].reshape(head_ref.shape[1:])
    each = LANES // bias_width
    for index in range(taps_ref.shape[0] // each):
        row = [
            taps_ref[order.index(index * each + i), fr // 2, fr % 2 : fr % 2 + 1, :bias_width].astype(f32)
            for i in range(each)
        ]
        row = row[0] if each == 1 else jnp.concatenate(row, axis=1)
        bias_ref[:, index * LANES : (index + 1) * LANES] = row


def span_kernel(
    fr,
    gsize,
    owner_ref,
    own_stack_ref,
    peer_stack_ref,
    own_head_ref,
    peer_head_ref,
    input_ref,
    bias_ref,
    extra_ref,
    pool_ref,
    line_ref,
    source_ref,
):
    blk = lax.axis_index("blk")
    core = lax.rem(blk, 2)
    n_chip, page, width = own_stack_ref.shape
    n_blk = 2 * n_chip
    pool_ref[...] = jnp.zeros_like(pool_ref)
    for chip in range(n_chip):
        for stack, side in ((own_stack_ref, core), (peer_stack_ref, 1 - core)):
            number = 2 * chip + side
            value = stack[chip]
            source_ref[number] = value
            owner = owner_ref[number]
            rank = jnp.int32(0)
            for other in range(n_blk):
                earlier = (owner_ref[other] == owner) & (other < number)
                rank = rank + earlier.astype(jnp.int32)

            @pl.when(owner == blk)
            def _(value=value, rank=rank):
                pool_ref[rank] = value

    groups = own_head_ref.shape[2]
    lanes = line_ref.shape[1]
    top_lag = blk * page + page - 1
    for head, side in ((own_head_ref, core), (peer_head_ref, 1 - core)):
        at = pl.multiple_of(side * groups, groups)
        line_ref[pl.ds(at, groups), :] = reversed_taps(head[...], 0, fr, top_lag, lanes)
    per = LANES // gsize
    for index in range(width // LANES):
        columns = slice(index * LANES, (index + 1) * LANES)
        source = source_ref[:, :, columns].reshape(n_blk * page, LANES)
        total = toeplitz_product(line_ref, index * per, gsize, page, n_blk * page, source)
        skip = bias_ref[:, columns] * input_ref[:, columns].astype(f32)
        extra_ref[:, columns] = total + skip


def finish_kernel(parts_ref, gate_ref, extra_ref, mixed_ref):
    n_blk, _, half = parts_ref.shape
    for core in range(2):
        columns = slice(core * half, (core + 1) * half)
        total = extra_ref[:, columns]
        for place, block in enumerate(part_order(n_blk)):
            if block % 2 == core:
                total = total + parts_ref[place].astype(f32)
        gate = gate_ref[:, columns].astype(f32)
        mixed_ref[:, columns] = (gate * total).astype(bf16)


def whole(memory=pltpu.VMEM):
    return pl.BlockSpec(memory_space=memory)


def limit(mebibytes):
    return pltpu.CompilerParams(vmem_limit_bytes=mebibytes << 20)


def per_device(
    history_u, span_gate, span_key, span_value, filter_taps, skip_bias, lengths, page_owner
):
    n_blk, n_ten = lax.axis_size("blk"), lax.axis_size("tenant")
    n_dev, n_chip = n_blk * n_ten, n_blk // 2
    history = history_u[0]
    rows, width = history.shape
    half = width // 2
    span_rows = span_key.shape[1]
    span = span_rows * n_blk
    fr, groups = filter_taps.shape
    gsize = width // groups
    pairs = round_up(fr + 1, 2) // 2
    bias_width = skip_bias.shape[0]
    swap = [(i, i ^ 1) for i in range(n_blk)]

    send, token = pl.pallas_call(
        functools.partial(pack_kernel, tap_order(n_blk, n_ten), n_ten),
        out_shape=(
            jax.ShapeDtypeStruct((n_dev, pairs, 2, groups // 2), bf16),
            jax.ShapeDtypeStruct((8, LANES), f32),
        ),
        in_specs=[whole(pltpu.HBM)] * 2,
        out_specs=(whole(), whole()),
        scratch_shapes=[
            pltpu.VMEM((fr, groups), bf16),
            pltpu.VMEM((1, bias_width), bf16),
            pltpu.SemaphoreType.DMA((2,)),
        ],
        compiler_params=limit(58),
        name="pack",
    )(filter_taps, skip_bias.reshape(1, bias_width))
    taps = lax.all_to_all(
        send,
        ("blk", "tenant"),
        split_axis=0,
        concat_axis=0,
        axis_index_groups=[tap_order(n_blk, n_ten)],
        tiled=True,
    )
    pieces = 4
    piece = rows // pieces
    peer_history = [
        lax.ppermute(history[i * piece : (i + 1) * piece], "blk", swap) for i in range(pieces)
    ]

    def half_block(count):
        return pl.BlockSpec((count, half), lambda i, n: (0, lax.rem(lax.axis_index("blk"), 2)))

    source = pl.pallas_call(
        source_kernel,
        grid_spec=pltpu.PrefetchScalarGridSpec(
            num_scalar_prefetch=1,
            grid=(1,),
            in_specs=[half_block(rows)] + [half_block(piece)] * pieces,
            out_specs=pl.BlockSpec((2 * rows, half), lambda i, n: (0, 0)),
        ),
        out_shape=jax.ShapeDtypeStruct((2 * rows, half), bf16),
        compiler_params=limit(8),
        name="source",
    )(lengths, history, *peer_history)

    inputs = pl.pallas_call(
        input_kernel,
        out_shape=jax.ShapeDtypeStruct((span_rows, width), bf16),
        in_specs=[whole(pl.ANY)] + [whole()] * 2,
        out_specs=whole(),
        compiler_params=limit(8),
        cost_estimate=pl.CostEstimate(flops=32768, bytes_accessed=3 * span_rows * width * 2, transcendentals=0),
        name="inputs",
    )(source, span_key[0], span_value[0])

    pages = [inputs]
    for step in range(1, n_chip):
        turn = [(i, i ^ (2 * step)) for i in range(n_blk)]
        pages.append(lax.ppermute(inputs, "blk", turn))
    partial = pl.pallas_call(
        functools.partial(conv_kernel, fr, n_ten, gsize),
        out_shape=jax.ShapeDtypeStruct((n_blk, span_rows, half), bf16),
        in_specs=[whole(pltpu.SMEM), whole(), whole()],
        out_specs=whole(pltpu.HBM),
        scratch_shapes=[
            pltpu.VMEM((groups // 2, round_up(2 * rows + span - 1, LANES)), f32),
            pltpu.VMEM((n_blk, span_rows, half), bf16),
            pltpu.SemaphoreType.DMA((OUT_COPIES,)),
        ],
        compiler_params=limit(16),
        name="conv",
    )(lengths, taps, source)

    partial, *pages = lax.optimization_barrier((partial, *pages))
    parts = lax.all_to_all(
        partial,
        "blk",
        split_axis=0,
        concat_axis=0,
        axis_index_groups=[part_order(n_blk)],
        tiled=True,
    )

    stack = jax.ShapeDtypeStruct((n_chip, span_rows, width), bf16)
    head = jax.ShapeDtypeStruct((min(n_dev, -(-span // fr)), 2 * pairs, groups // 2), bf16)
    own_stack, own_head, bias = pl.pallas_call(
        functools.partial(gather_kernel, tap_order(n_blk, n_ten), fr, bias_width),
        out_shape=(stack, head, jax.ShapeDtypeStruct((1, width), f32)),
        in_specs=[whole(pl.ANY)] + [whole()] * (1 + n_chip),
        out_specs=(whole(),) * 3,
        compiler_params=limit(8),
        name="gather",
    )(partial, taps, *pages)
    peer_stack = lax.ppermute(own_stack, "blk", swap)
    peer_head = lax.ppermute(own_head, "blk", swap)

    extra, pool = pl.pallas_call(
        functools.partial(span_kernel, fr, gsize),
        out_shape=(
            jax.ShapeDtypeStruct((span_rows, width), f32),
            jax.ShapeDtypeStruct((MOST, PAGE, width), bf16),
        ),
        in_specs=[whole(pltpu.SMEM)] + [whole()] * 6,
        out_specs=(whole(), whole()),
        scratch_shapes=[
            pltpu.VMEM((groups, round_up(span + PAGE - 1, LANES)), f32),
            pltpu.VMEM((n_blk, span_rows, width), bf16),
        ],
        compiler_params=limit(8),
        name="span",
    )(page_owner.reshape(n_blk), own_stack, peer_stack, own_head, peer_head, inputs, bias)

    mixed = pl.pallas_call(
        finish_kernel,
        out_shape=jax.ShapeDtypeStruct((span_rows, width), bf16),
        in_specs=[whole()] * 3,
        out_specs=whole(),
        compiler_params=limit(8),
        name="finish",
    )(parts, span_gate[0], extra)
    return mixed[None], pool.reshape(1, MOST * PAGE, width)


def solution(mesh):
    return jax.shard_map(
        per_device,
        mesh=mesh,
        in_specs=(
            P("tenant", "blk", None),
            P("tenant", "blk", None),
            P("tenant", "blk", None),
            P("tenant", "blk", None),
            P(("blk", "tenant"), None),
            P(("blk", "tenant")),
            P("tenant"),
            P("tenant", None, None),
        ),
        out_specs=(P("tenant", "blk", None), P("tenant", "blk", None)),
        check_vma=False,
    )
```
